32 devices in a mesh: level: 2 (over x), tile: 16 (over z, y, core).
Axes of the slice: x: 2, y: 2, z: 4, core: 2. Of those that a mesh axis runs over, the one named last changes fastest.
Arguments:
- density: float32 [2, 8, 8, 8, 2048], P('level', None, None, None, 'tile'), may hold values from 1 to 2
- momentum: float32 [2, 3, 8, 8, 8, 2048], P('level', None, None, None, None, 'tile'), may hold values from -0.3 to 0.3
- energy: float32 [2, 8, 8, 8, 2048], P('level', None, None, None, 'tile'), may hold values from 2.5 to 3.5
- rhs_older: float32 [2, 5, 8, 8, 8, 2048], P('level', None, None, None, None, 'tile'), may hold values from -4.5 to 4.5
- rhs_old: float32 [2, 5, 8, 8, 8, 2048], P('level', None, None, None, None, 'tile'), may hold values from -4.5 to 4.5
- peer_tile: int32 [16, 120], P('tile'), may hold values from 0 to 15, as said below
- peer_index: int32 [16, 120], P('tile'), may hold values from 0 to 119, as said below
- boundary_slot: int32 [16, 120], P('tile'), may hold values from 0 to 767, as said below
- face_partner: int32 [16, 768], P('tile'), may hold values from 0 to 767, as said below
- face_orient: int32 [16, 768], P('tile'), may hold values from 0 to 3, as said below
Outputs:
- tendency: float32 [2, 5, 8, 8, 8, 2048], P('level', None, None, None, None, 'tile')
The draws below stay inside these ranges and needn't reach their ends.
Inputs may be any that keep to these rules, and one draw needn't show every extreme that they name: `peer_tile`: never the tile itself; the partner's partner is the face itself; every two distinct tiles share exactly 8 face pairs. `peer_index`: consistent with peer_tile: the partner face's own entries point back to this face. `boundary_slot`: distinct within a tile, and these slots are exactly the slots that face_partner maps to themselves. `face_partner`: symmetric within a tile: slots not on the boundary come in pairs that name each other; boundary slots name themselves. `face_orient`: equal at both faces of every pair, within a tile and across tiles.
All inputs are finite; a program needn't handle non-finite values.
Results may differ from the reference program's by a relative error of at most 0.0001.
Values sent between devices are 32-bit elements; how exact they have to be, the bound alone decides.
A program may use at most 384 MiB of HBM per device.

```python
import jax
import jax.numpy as jnp
import numpy as np
from jax import lax

NP = 8
TSTEPS = 3
FCAP = 8
LEVELS = 2
TILES = 16
ELEMENTS = 2048
FACES = 768
FB = 120


def connectivity(key):
    base = jax.random.fold_in(key, 11)
    streams = jax.random.split(base, 7)
    rounds = FB // FCAP
    masks = jax.random.permutation(streams[0], TILES - 1)[:rounds] + 1
    position = jnp.arange(FB)
    round_of = position // FCAP
    mask_of = masks[round_of]
    relabel = jax.random.permutation(streams[2], TILES)
    restore = jnp.argsort(relabel)
    ordering = jax.vmap(lambda stream: jax.random.permutation(stream, FB))(jax.random.split(streams[3], TILES))
    unorder = jnp.argsort(ordering, axis=1)
    rows = jnp.arange(TILES)[:, None]
    other = jnp.bitwise_xor(rows, mask_of[unorder])
    tile_rel = relabel[other]
    index_rel = ordering[other, unorder]
    pair_table = jax.random.randint(streams[4], (TILES, FB), 0, 4)
    orient_rel = pair_table[jnp.minimum(rows, other), unorder]
    slot_perm = jax.vmap(lambda stream: jax.random.permutation(stream, FACES))(jax.random.split(streams[5], TILES))
    peer_tile = tile_rel[restore].astype(jnp.int32)
    peer_index = index_rel[restore].astype(jnp.int32)
    boundary_orient = orient_rel[restore].astype(jnp.int32)
    boundary_slot = slot_perm[:, :FB].astype(jnp.int32)
    left = slot_perm[:, FB::2]
    right = slot_perm[:, FB + 1::2]
    partner = jnp.broadcast_to(jnp.arange(FACES, dtype=jnp.int32), (TILES, FACES))
    partner = partner.at[rows, left].set(right.astype(jnp.int32)).at[rows, right].set(left.astype(jnp.int32))
    inner_orient = jax.random.randint(streams[6], (TILES, (FACES - FB) // 2), 0, 4).astype(jnp.int32)
    orient = jnp.zeros((TILES, FACES), jnp.int32)
    orient = orient.at[rows, left].set(inner_orient).at[rows, right].set(inner_orient)
    orient = orient.at[rows, boundary_slot].set(boundary_orient)
    return (peer_tile, peer_index, boundary_slot, partner, orient)


def draw_peer_tile(key, part):
    return connectivity(key)[0]


def draw_peer_index(key, part):
    return connectivity(key)[1]


def draw_boundary_slot(key, part):
    return connectivity(key)[2]


def draw_face_partner(key, part):
    return connectivity(key)[3]


def draw_face_orient(key, part):
    return connectivity(key)[4]


def level_of(own_key, extent, cuts, smallest, largest):
    gain = 1.0
    for axis_at, shards_of in cuts:
        steps = jax.random.uniform(jax.random.fold_in(jax.random.fold_in(own_key, 6), axis_at), (shards_of,), jnp.float32, smallest / len(cuts), largest / len(cuts))
        gain = gain * jnp.repeat(jnp.exp(steps), extent[axis_at] // shards_of).reshape((-1,) + (1,) * (len(extent) - 1 - axis_at))
    return gain


def gaussian(stream_key, dims, scale, reach, cuts=(), kind=jnp.bfloat16):
    array = jax.random.normal(stream_key, dims, jnp.float32) * scale
    if len(cuts) > 0:
        array = level_of(stream_key, dims, cuts, -0.22, 0.18) * array
    return jnp.clip(array, min=-reach, max=reach).astype(kind)


def setup_inputs(seed: int = 0) -> dict:
    arg_keys = jax.random.split(jax.random.key(seed), 11)
    return {
        "density": jnp.clip(1.0 + 1.0 * jax.random.uniform(arg_keys[0], (LEVELS, NP, NP, NP, ELEMENTS), jnp.float32) ** level_of(arg_keys[0], (LEVELS, NP, NP, NP, ELEMENTS), ((0, 2), (4, 16)), -0.2, 0.2), 1.0, 2.0),
        "momentum": jnp.clip(jax.random.uniform(arg_keys[1], (LEVELS, 3, NP, NP, NP, ELEMENTS), jnp.float32, -0.3, 0.3) * level_of(arg_keys[1], (LEVELS, 3, NP, NP, NP, ELEMENTS), ((0, 2), (5, 16)), -0.4, 0.0), -0.3, 0.3),
        "energy": jnp.clip(2.5 + 1.0 * jax.random.uniform(arg_keys[2], (LEVELS, NP, NP, NP, ELEMENTS), jnp.float32) ** level_of(arg_keys[2], (LEVELS, NP, NP, NP, ELEMENTS), ((0, 2), (4, 16)), -0.2, 0.2), 2.5, 3.5),
        "rhs_older": gaussian(arg_keys[3], (LEVELS, 5, NP, NP, NP, ELEMENTS), 1.5, 4.5, ((0, 2), (5, 16)), jnp.float32),
        "rhs_old": gaussian(arg_keys[4], (LEVELS, 5, NP, NP, NP, ELEMENTS), 1.5, 4.5, ((0, 2), (5, 16)), jnp.float32),
        "peer_tile": draw_peer_tile(jax.random.fold_in(arg_keys[10], 71), 0),
        "peer_index": draw_peer_index(jax.random.fold_in(arg_keys[10], 71), 0),
        "boundary_slot": draw_boundary_slot(jax.random.fold_in(arg_keys[10], 71), 0),
        "face_partner": draw_face_partner(jax.random.fold_in(arg_keys[10], 71), 0),
        "face_orient": draw_face_orient(jax.random.fold_in(arg_keys[10], 71), 0),
    }


step_size = 0.02
penalty = 2.5
metric = 0.1
lift_factor = 2.8
weight_back = -1.0 / 12.0
weight_here = 8.0 / 12.0
weight_next = 5.0 / 12.0


def lobatto_points():
    degree = NP - 1
    points = np.cos(np.pi * np.arange(degree + 1) / degree)
    table = np.zeros((degree + 1, degree + 1))
    for sweep in range(60):
        table[:, 0] = 1.0
        table[:, 1] = points
        for order in range(2, degree + 1):
            table[:, order] = ((2 * order - 1) * points * table[:, order - 1] - (order - 1) * table[:, order - 2]) / order
        points = points - (points * table[:, degree] - table[:, degree - 1]) / ((degree + 1) * table[:, degree])
    table[:, 0] = 1.0
    table[:, 1] = points
    for order in range(2, degree + 1):
        table[:, order] = ((2 * order - 1) * points * table[:, order - 1] - (order - 1) * table[:, order - 2]) / order
    return points[::-1], table[::-1, degree]


def derivative_table():
    degree = NP - 1
    points, values = lobatto_points()
    identity = np.eye(NP)
    spread = points[:, None] - points[None, :] + identity
    table = values[:, None] / values[None, :] / spread
    table = table * (1.0 - identity)
    table[0, 0] = -degree * (degree + 1) / 4.0
    table[degree, degree] = degree * (degree + 1) / 4.0
    return jnp.asarray(table, dtype=jnp.float32)


def directional_flux(state, direction):
    density_part = state[0]
    momenta = state[1:4]
    energy_part = state[4]
    velocity = momenta / density_part
    pressure = 0.4 * (energy_part - 0.5 * (momenta[0] * velocity[0] + momenta[1] * velocity[1] + momenta[2] * velocity[2]))
    carried = momenta[direction]
    pieces = [carried]
    for column in range(3):
        product = carried * velocity[column]
        if column == direction:
            product = product + pressure
        pieces.append(product)
    pieces.append((energy_part + pressure) * velocity[direction])
    return jnp.stack(pieces)


def face_traces(state, tiles):
    planes = []
    for which in range(6):
        direction = which // 2
        plane = jnp.take(state, (NP - 1) * (which % 2), axis=2 + direction)
        planes.append(plane.reshape(plane.shape[:4] + (tiles, plane.shape[4] // tiles)))
    stacked = jnp.stack(planes, axis=5)
    return stacked.reshape(stacked.shape[:4] + (-1,))


def oriented(raw, orient):
    turned = raw[:, :, ::-1, ::-1, :]
    first = jnp.where(orient >= 2, turned, raw)
    second = jnp.swapaxes(first, 2, 3)
    return jnp.where(orient % 2 == 1, second, first)


def tendency_of(state, partner_view, tiles):
    table = derivative_table()
    highest = lax.Precision.HIGHEST
    volume = jnp.einsum('ai,vbijke->vbajke', table, directional_flux(state, 0), precision=highest)
    volume = volume + jnp.einsum('aj,vbijke->vbiake', table, directional_flux(state, 1), precision=highest)
    volume = volume + jnp.einsum('ak,vbijke->vbijae', table, directional_flux(state, 2), precision=highest)
    result = -metric * volume
    traces = face_traces(state, tiles)
    view = partner_view(traces)
    grouped = traces.shape[:4] + (tiles, 6, -1)
    own_all = traces.reshape(grouped)
    far_all = view.reshape(grouped)
    for which in range(6):
        direction = which // 2
        normal = 2.0 * (which % 2) - 1.0
        own = own_all[:, :, :, :, :, which].reshape(traces.shape[:4] + (-1,))
        far = far_all[:, :, :, :, :, which].reshape(traces.shape[:4] + (-1,))
        jump = 0.5 * normal * (directional_flux(far, direction) - directional_flux(own, direction)) - 0.5 * penalty * (far - own)
        location = (slice(None),) * (2 + direction) + ((NP - 1) * (which % 2),)
        result = result.at[location].add(-lift_factor * jump)
    return result


def reference(density, momentum, energy, rhs_older, rhs_old, peer_tile, peer_index, boundary_slot, face_partner, face_orient):
    start = jnp.concatenate([density[:, None], momentum, energy[:, None]], axis=1)
    offsets = (jnp.arange(TILES, dtype=jnp.int32) * FACES)[:, None]
    inner_source = (offsets + face_partner).reshape(-1)
    target = (offsets + boundary_slot).reshape(-1)
    remote_slot = boundary_slot[peer_tile, peer_index]
    remote_source = (peer_tile * FACES + remote_slot).reshape(-1)
    gather_index = inner_source.at[target].set(remote_source)
    orient_flat = face_orient.reshape(-1)

    def partner_view(traces):
        return oriented(traces[..., gather_index], orient_flat)

    def level_rate(level_state):
        return tendency_of(level_state[:, None], partner_view, TILES)[:, 0]

    levels = jnp.arange(LEVELS, dtype=jnp.int32).reshape(-1, 1, 1, 1, 1, 1)
    state = start
    older = rhs_older
    old = rhs_old
    for repeat in range(TSTEPS):
        own_rate = lax.map(level_rate, state)
        below = jnp.concatenate([jnp.zeros_like(own_rate[:1]), own_rate[:-1]], axis=0)
        corrected = state + step_size * (own_rate - old) + step_size * (weight_back * older + weight_here * old + weight_next * below)
        predicted = state + step_size * own_rate
        state = jnp.where(levels == 0, predicted, corrected)
        older = old
        old = below
    return (state - start) / (TSTEPS * step_size)
```

```python
import functools

import jax
import jax.numpy as jnp
import numpy as np
from jax import lax
from jax.experimental import pallas as pl
from jax.experimental.pallas import tpu as pltpu
from jax.sharding import PartitionSpec as P

NP = 8
TSTEPS = 3
FCAP = 8


step_size = 0.02
penalty = 2.5
metric = 0.1
lift_factor = 2.8
weight_back = -1.0 / 12.0
weight_here = 8.0 / 12.0
weight_next = 5.0 / 12.0


def shifted(block, axis, distance):
    devices = range(lax.axis_size(axis))
    route = [(i - distance, i) for i in devices if i - distance in devices]
    return lax.ppermute(block, axis, route)


def lobatto_points():
    degree = NP - 1
    points = np.cos(np.pi * np.arange(degree + 1) / degree)
    table = np.zeros((degree + 1, degree + 1))
    for sweep in range(60):
        table[:, 0] = 1.0
        table[:, 1] = points
        for order in range(2, degree + 1):
            table[:, order] = (
                (2 * order - 1) * points * table[:, order - 1] - (order - 1) * table[:, order - 2]
            ) / order
        points = points - (points * table[:, degree] - table[:, degree - 1]) / (
            (degree + 1) * table[:, degree]
        )
    table[:, 0] = 1.0
    table[:, 1] = points
    for order in range(2, degree + 1):
        table[:, order] = (
            (2 * order - 1) * points * table[:, order - 1] - (order - 1) * table[:, order - 2]
        ) / order
    return (points[::-1], table[::-1, degree])


def derivative_numbers():
    degree = NP - 1
    points, values = lobatto_points()
    identity = np.eye(NP)
    spread = points[:, None] - points[None, :] + identity
    table = values[:, None] / values[None, :] / spread
    table = table * (1.0 - identity)
    table[0, 0] = -degree * (degree + 1) / 4.0
    table[degree, degree] = degree * (degree + 1) / 4.0
    return np.asarray(table, dtype=np.float32)

NV = 5
NODES = NP * NP
ROWS = NV * NODES
SIZE = NV * NP * NODES
CELLS = NP * NODES
STEPS = 8
SCALE = 1.0 / (TSTEPS * step_size)


def primitive(w):
    inverse = 1.0 / w[0]
    velocity = [w[c] * inverse for c in (1, 2, 3)]
    pressure = 0.4 * (w[4] - 0.5 * (w[1] * velocity[0] + w[2] * velocity[1] + w[3] * velocity[2]))
    return velocity, pressure


def flux(w, velocity, pressure, direction):
    carried = w[1 + direction]
    parts = [carried]
    for column in range(3):
        product = carried * velocity[column]
        if column == direction:
            product = product + pressure
        parts.append(product)
    parts.append((w[4] + pressure) * velocity[direction])
    return parts


def pieces_of(x):
    high = x.astype(jnp.bfloat16)
    rest = x - high.astype(jnp.float32)
    middle = rest.astype(jnp.bfloat16)
    low = (rest - middle.astype(jnp.float32)).astype(jnp.bfloat16)
    return [high, middle, low]


def face_rows(which):
    direction, end = which // 2, (NP - 1) * (which % 2)
    return direction, end


def trace_rows(ref, which, v):
    direction, end = face_rows(which)
    base = v * NP * NODES
    if direction == 0:
        return ref[pl.ds(base + end * NODES, NODES), :]
    if direction == 1:
        return jnp.concatenate(
            [ref[pl.ds(base + i * NODES + end * NP, NP), :] for i in range(NP)], axis=0
        )
    return ref[pl.ds(base + end, NODES, stride=NP), :]


def gather_traces(state, masks, turn, turned):
    width = state.shape[1]
    for which in range(6):
        lanes = pl.ds(which * width, width)
        mask = [jnp.broadcast_to(masks[o : o + 1, lanes], (NODES, width)) for o in range(4)]
        for v in range(NV):
            for at, piece in enumerate(pieces_of(trace_rows(state, which, v))):
                wide = piece.astype(jnp.float32)
                stacked = jnp.concatenate([(wide * m).astype(jnp.bfloat16) for m in mask], axis=0)
                out = jnp.dot(turn[...], stacked, preferred_element_type=jnp.float32)
                turned[at, pl.ds(v * NODES, NODES), lanes] = out.astype(jnp.bfloat16)


def outgoing_of(turned, send):
    outgoing = None
    for at in range(3):
        leave = lax.dot_general(
            send[...], turned[at], (((1,), (1,)), ((), ())), preferred_element_type=jnp.float32
        )
        outgoing = leave if outgoing is None else outgoing + leave
    return outgoing


def inner_of(turned, inner):
    total = None
    for at in range(3):
        part = jnp.dot(turned[at], inner[...], preferred_element_type=jnp.float32)
        total = part if total is None else total + part
    return total


def outer_of(arrived, place):
    total = None
    for piece in pieces_of(arrived):
        part = lax.dot_general(
            piece, place[...], (((0,), (0,)), ((), ())), preferred_element_type=jnp.float32
        )
        total = part if total is None else total + part
    return total


def volume_of(state, rolled, rate):
    numbers = derivative_numbers()

    def derived(fields):
        even = [fields[index] + fields[NP - 1 - index] for index in range(NP // 2)]
        odd = [fields[index] - fields[NP - 1 - index] for index in range(NP // 2)]
        results = [None] * NP
        for target in range(NP // 2):
            near = None
            far = None
            for index in range(NP // 2):
                here = float(numbers[target, index])
                there = float(numbers[target, NP - 1 - index])
                one = (-0.5 * metric * (here + there)) * even[index]
                two = (-0.5 * metric * (here - there)) * odd[index]
                near = one if near is None else near + one
                far = two if far is None else far + two
            results[target] = far + near
            results[NP - 1 - target] = far - near
        return results

    def at(v, i, j):
        return pl.ds(pl.multiple_of(v * NP * NODES + i * NODES + j * NP, NP), NP)

    def along_first(j, carry):
        across = [[None] * NP for v in range(NV)]
        down = [[None] * NP for v in range(NV)]
        for i in range(NP):
            w = [state[at(v, i, j), :] for v in range(NV)]
            velocity, pressure = primitive(w)
            for v, part in enumerate(flux(w, velocity, pressure, 0)):
                across[v][i] = part
            for v, part in enumerate(flux(w, velocity, pressure, 2)):
                total = rolled[0] * part
                for shift in range(1, NP):
                    total = total + rolled[shift] * pltpu.roll(part, NP - shift, 0)
                down[v][i] = total
        for v in range(NV):
            for i, part in enumerate(derived(across[v])):
                rate[at(v, i, j), :] = part + down[v][i]
        return carry

    def along_second(i, carry):
        across = [[None] * NP for v in range(NV)]
        for j in range(NP):
            w = [state[at(v, i, j), :] for v in range(NV)]
            velocity, pressure = primitive(w)
            for v, part in enumerate(flux(w, velocity, pressure, 1)):
                across[v][j] = part
        for v in range(NV):
            for j, part in enumerate(derived(across[v])):
                rate[at(v, i, j), :] = rate[at(v, i, j), :] + part
        return carry

    lax.fori_loop(0, NP, along_first, 0)
    lax.fori_loop(0, NP, along_second, 0)


def lift_faces(state, view, rate):
    width = state.shape[1]
    for which in range(6):
        direction, end = face_rows(which)
        normal = 2.0 * (which % 2) - 1.0
        lanes = pl.ds(which * width, width)

        def lift(row, carry):
            def rows(v):
                base = v * NP * NODES
                if direction == 0:
                    return pl.ds(pl.multiple_of(base + end * NODES + row * NP, NP), NP)
                if direction == 1:
                    return pl.ds(pl.multiple_of(base + row * NODES + end * NP, NP), NP)
                return pl.ds(base + row * NODES + end, NP, stride=NP)

            own = [state[rows(v), :] for v in range(NV)]
            far = [
                view[pl.ds(pl.multiple_of(v * NODES + row * NP, NP), NP), lanes]
                for v in range(NV)
            ]
            own_flux = flux(own, *primitive(own), direction)
            far_flux = flux(far, *primitive(far), direction)
            for v in range(NV):
                jump = (0.5 * normal) * (far_flux[v] - own_flux[v]) - (0.5 * penalty) * (
                    far[v] - own[v]
                )
                rate[rows(v), :] = rate[rows(v), :] - lift_factor * jump
            return carry

        lax.fori_loop(0, NP, lift, 0)


VMEM = pl.BlockSpec(memory_space=pltpu.VMEM)


def rate_kernel(count, *refs):
    states, refs = refs[:count], refs[count:]
    masks, turn, inner, send, place, rolled = refs[:6]
    rates, refs = refs[6 : 6 + count], refs[6 + count :]
    turned, views, buffer, landed, send_sem, recv_sem = refs
    tiles = lax.axis_size("tile")
    me = lax.axis_index("tile")
    barrier = pltpu.get_barrier_semaphore()

    def peer(offset):
        return {"tile": lax.rem(me + offset, tiles)}

    def copy(offset):
        return pltpu.make_async_remote_copy(
            src_ref=buffer.at[lax.rem(me + offset, tiles)],
            dst_ref=landed.at[me],
            send_sem=send_sem.at[offset],
            recv_sem=recv_sem.at[offset],
            device_id=peer(offset),
            device_id_type=pl.DeviceIdType.MESH,
        )

    def greet(offset, carry):
        pl.semaphore_signal(
            barrier, inc=1, device_id=peer(offset), device_id_type=pl.DeviceIdType.MESH
        )
        return carry

    def begin(offset, carry):
        copy(offset).start()
        return carry

    def finish(offset, carry):
        copy(offset).wait()
        return carry

    lax.fori_loop(1, tiles, greet, 0)
    for at in range(count):
        gather_traces(states[at], masks, turn, turned.at[at])
        leave = outgoing_of(turned.at[at], send)
        buffer[:, at * FCAP : (at + 1) * FCAP, :] = leave.reshape(tiles, FCAP, ROWS)
    pl.semaphore_wait(barrier, tiles - 1)
    lax.fori_loop(1, tiles, begin, 0)
    landed[me] = jnp.zeros(landed.shape[1:], jnp.float32)
    for at in range(count):
        views[at] = inner_of(turned.at[at], inner)
        volume_of(states[at], rolled, rates[at])
    lax.fori_loop(1, tiles, finish, 0)
    for at in range(count):
        arrived = landed[:, at * FCAP : (at + 1) * FCAP, :].reshape(tiles * FCAP, ROWS)
        views[at] = views[at] + outer_of(arrived, place)
        lift_faces(states[at], views.at[at], rates[at])


def rates_of(states, tables):
    tiles = lax.axis_size("tile")
    count = len(states)
    slots = tables[0].shape[1]
    like = jax.ShapeDtypeStruct(states[0].shape, jnp.float32)
    return pl.pallas_call(
        functools.partial(rate_kernel, count),
        out_shape=[like] * count,
        in_specs=[VMEM] * (count + len(tables)),
        out_specs=[VMEM] * count,
        scratch_shapes=[
            pltpu.VMEM((count, 3, ROWS, slots), jnp.bfloat16),
            pltpu.VMEM((count, ROWS, slots), jnp.float32),
            pltpu.VMEM((tiles, count * FCAP, ROWS), jnp.float32),
            pltpu.VMEM((tiles, count * FCAP, ROWS), jnp.float32),
            pltpu.SemaphoreType.DMA((tiles,)),
            pltpu.SemaphoreType.DMA((tiles,)),
        ],
        compiler_params=pltpu.CompilerParams(
            collective_id=count - 1, has_side_effects=True, vmem_limit_bytes=40 << 20
        ),
    )(*states, *tables)


def pieces_pair(x):
    high = x.astype(jnp.bfloat16)
    return high, (x - high.astype(jnp.float32)).astype(jnp.bfloat16)


def fluxes(w):
    inverse = 1.0 / w[0]
    velocity = [w[c] * inverse for c in (1, 2, 3)]
    product = {}
    for a in range(3):
        for b in range(a, 3):
            product[a, b] = product[b, a] = w[1 + a] * velocity[b]
    pressure = 0.4 * (w[4] - 0.5 * (product[0, 0] + product[1, 1] + product[2, 2]))
    total = w[4] + pressure
    return [
        [w[1 + d]]
        + [product[d, c] + pressure if c == d else product[d, c] for c in range(3)]
        + [total * velocity[d]]
        for d in range(3)
    ]


def derived(fields):
    numbers = derivative_numbers()
    even = [fields[index] + fields[NP - 1 - index] for index in range(NP // 2)]
    odd = [fields[index] - fields[NP - 1 - index] for index in range(NP // 2)]
    results = [None] * NP
    for target in range(NP // 2):
        near = None
        far = None
        for index in range(NP // 2):
            here = float(numbers[target, index])
            there = float(numbers[target, NP - 1 - index])
            one = (-0.5 * metric * (here + there)) * even[index]
            two = (-0.5 * metric * (here - there)) * odd[index]
            near = one if near is None else near + one
            far = two if far is None else far + two
        results[target] = far + near
        results[NP - 1 - target] = far - near
    return results


HALF = NP * NODES // 2


def block_numbers():
    whole = np.kron(np.eye(HALF // NP), -metric * derivative_numbers()).astype(np.float32)
    high = whole.astype(jnp.bfloat16)
    low = (whole - high.astype(np.float32)).astype(jnp.bfloat16)
    return np.concatenate([high, low, high], axis=1)


def spread_traces(state, spread):
    width = state.shape[1]
    for which in range(6):
        lanes = pl.ds(which * width, width)
        for v in range(NV):
            high, low = pieces_pair(trace_rows(state, which, v))
            spread[pl.ds(v * NODES, NODES), lanes] = high
            spread[pl.ds(ROWS + v * NODES, NODES), lanes] = low


def node_rows(v, i, j, count=NP):
    return pl.ds(v * NP * NODES + i * NODES + j * NP, count)


def planes_and_views(state, spread, inner, flow, high, low, rate, view):
    width = state.shape[1]
    for i in range(NP):
        across = [[None] * NP for v in range(NV)]
        for j in range(0, NP, 2):
            thirds = [None, None]
            for half in range(2):
                w = [state[node_rows(v, i, j + half), :] for v in range(NV)]
                one, two, thirds[half] = fluxes(w)
                for v in range(NV):
                    across[v][j + half] = two[v]
                    flow[node_rows(v, i, j + half), :] = one[v]
            for v in range(NV):
                both = jnp.concatenate([thirds[0][v], thirds[1][v]], axis=0)
                upper, lower = pieces_pair(both)
                high[node_rows(v, i, j, 2 * NP), :] = upper
                low[node_rows(v, i, j, 2 * NP), :] = lower
        for v in range(NV):
            for j, part in enumerate(derived(across[v])):
                rate[node_rows(v, i, j), :] = part
        if i % 2 == 0 and i < 6:
            both = jnp.dot(
                spread[...], inner[:, i * width : (i + 2) * width],
                preferred_element_type=jnp.float32,
            )
            both = both[:ROWS] + both[ROWS:]
            for half in range(2):
                view[pl.ds((i + half) * ROWS, ROWS), :] = both[:, half * width : (half + 1) * width]


def remaining_volume(flow, high, low, blocks, rate):
    width = flow.shape[1]
    for v in range(NV):
        base = v * NP * NODES

        def pair(ref):
            return jnp.concatenate(
                [ref[pl.ds(base, HALF), :], ref[pl.ds(base + HALF, HALF), :]], axis=1
            )

        upper, lower = pair(high), pair(low)
        down = jnp.dot(
            blocks[...],
            jnp.concatenate([upper, upper, lower], axis=0),
            preferred_element_type=jnp.float32,
        )
        for j in range(NP):
            parts = derived([flow[node_rows(v, i, j), :] for i in range(NP)])
            for i, part in enumerate(parts):
                row, lane = (i % 4) * NODES + j * NP, (i // 4) * width
                rows = node_rows(v, i, j)
                rate[rows, :] = rate[rows, :] + part + down[row : row + NP, lane : lane + width]


def lift_all(state, view, traces, place, orient, rate):
    width = state.shape[1]
    upper, lower = pieces_pair(traces.T)
    sides = jnp.concatenate([upper, lower], axis=0)
    ahead = lax.broadcasted_iota(jnp.int32, (NP, width), 0)
    for which in range(6):
        direction, end = face_rows(which)
        normal = 2.0 * (which % 2) - 1.0
        lanes = pl.ds(which * width, width)
        if which % 2 == 0:
            outer = jnp.dot(
                sides, place[:, which * width : (which + 2) * width],
                preferred_element_type=jnp.float32,
            )
            outer = outer[:ROWS] + outer[ROWS:]
            for half in range(2):
                rows = pl.ds((which + half) * ROWS, ROWS)
                view[rows, :] = view[rows, :] + outer[:, half * width : (half + 1) * width]
        orients = jnp.broadcast_to(orient[0:1, lanes], (NP, width))
        crossed = (orients & 1) == 1
        turned = orients >= 2
        order = jnp.where(turned, NP - 1 - ahead, ahead)

        def rows_of(v, row):
            base = v * NP * NODES
            if direction == 0:
                return pl.ds(base + end * NODES + row * NP, NP)
            if direction == 1:
                return pl.ds(base + row * NODES + end * NP, NP)
            return pl.ds(base + row * NODES + end, NP, stride=NP)

        for near in range(NP // 2):
            pair = [near, NP - 1 - near]
            far = [[], []]
            for v in range(NV):
                base = which * ROWS + v * NODES
                seen = [
                    jnp.where(
                        crossed,
                        view[pl.ds(base + row, NP, stride=NP), :],
                        view[pl.ds(base + row * NP, NP), :],
                    )
                    for row in pair
                ]
                for half in range(2):
                    picked = jnp.where(turned, seen[1 - half], seen[half])
                    far[half].append(
                        jnp.take_along_axis(picked, order, axis=0, mode="promise_in_bounds")
                    )
            for half in range(2):
                rows = [rows_of(v, pair[half]) for v in range(NV)]
                own = [state[rows[v], :] for v in range(NV)]
                own_flux = flux(own, *primitive(own), direction)
                far_flux = flux(far[half], *primitive(far[half]), direction)
                for v in range(NV):
                    jump = (0.5 * normal) * (far_flux[v] - own_flux[v]) - (0.5 * penalty) * (
                        far[half][v] - own[v]
                    )
                    rate[rows[v], :] = rate[rows[v], :] - lift_factor * jump


def table_rows(ref, fill):
    row = ref[...].astype(jnp.float32)
    extra = -row.shape[1] % 128
    if extra > 0:
        row = jnp.concatenate([row, jnp.full((1, extra), fill, jnp.float32)], axis=1)
    return row


def fill_tables(peers, matches, slots, partner, inner, send, place):
    faces = partner.shape[1]
    pack = 16

    def some(at, carry):
        base = pl.multiple_of(at * pack, pack)
        ids = lax.broadcasted_iota(jnp.int32, (pack, faces), 0) + base
        lane = lax.broadcasted_iota(jnp.int32, (pack, faces), 1)
        mate = jnp.broadcast_to(partner[...], (pack, faces))
        hit = jnp.where((ids == mate) & (mate != lane), 1.0, 0.0)
        inner[pl.ds(base, pack), :] = hit.astype(jnp.bfloat16)
        return carry

    lax.fori_loop(0, faces // pack, some, 0)
    peer = table_rows(peers, -1.0)
    match = table_rows(matches, -1.0)
    slot = table_rows(slots, -1.0)
    count = peer.shape[1]
    square = (count, count)
    peer_across = jnp.broadcast_to(peer, square)
    match_across = jnp.broadcast_to(match, square)
    same = peer_across.T == peer_across
    lower = match_across.T < match_across
    sooner = lax.broadcasted_iota(jnp.int32, square, 0) < lax.broadcasted_iota(jnp.int32, square, 1)
    slot_of = lax.broadcasted_iota(jnp.int32, (faces, count), 0).astype(jnp.float32)
    at_slot = jnp.where(slot_of == jnp.broadcast_to(slot, (faces, count)), 1.0, 0.0)
    at_slot = at_slot.astype(jnp.bfloat16)
    places = send.shape[0]
    spots = lax.broadcasted_iota(jnp.int32, (places, count), 0).astype(jnp.float32)
    for ahead, table in ((lower, send), (sooner, place)):
        rank = jnp.sum(jnp.where(same & ahead, 1.0, 0.0), axis=0, keepdims=True)
        spot = jnp.broadcast_to(peer * FCAP + rank, (places, count))
        onehot = jnp.where(spots == spot, 1.0, 0.0).astype(jnp.bfloat16)
        routed = lax.dot_general(
            onehot, at_slot, (((1,), (1,)), ((), ())), preferred_element_type=jnp.float32
        )
        table[...] = routed.astype(jnp.bfloat16)


def window_kernel(*refs):
    fields, refs = refs[:5], refs[5:]
    indices, refs = refs[:6], refs[6:]
    out, refs = refs[0], refs[1:]
    states, rates, older, old, refs = refs[0], refs[1], refs[2], refs[3], refs[4:]
    held, refs = refs[:6], refs[6:]
    inner, send, place, spread, flow, high, low, view, refs = *refs[:8], refs[8:]
    buffer, traces, send_sem, recv_sem, load_sem, table_sem, pass_send, pass_recv = refs
    peers, matches, slots, partner, orient, blocks = held
    tiles = lax.axis_size("tile")
    me = lax.axis_index("tile")
    level = lax.axis_index("level")
    base_level = level == 0
    upper = (level > 0).astype(jnp.float32)
    other = {"level": 1 - level}
    barrier = pltpu.get_barrier_semaphore()
    parts = [
        (fields[0], 0, CELLS),
        (fields[1], CELLS, 3 * CELLS),
        (fields[2], 4 * CELLS, CELLS),
    ]

    def peer(offset):
        return {"tile": lax.rem(me + offset, tiles)}

    def swap(stage, offset):
        return pltpu.make_async_remote_copy(
            src_ref=buffer.at[stage, lax.rem(me + offset, tiles)],
            dst_ref=traces.at[stage, me],
            send_sem=send_sem.at[stage, offset],
            recv_sem=recv_sem.at[stage, offset],
            device_id=peer(offset),
            device_id_type=pl.DeviceIdType.MESH,
        )

    def handed(at):
        ref, base, count = parts[at]
        return pltpu.make_async_remote_copy(
            src_ref=ref,
            dst_ref=states.at[2, pl.ds(base, count), :],
            send_sem=pass_send.at[at],
            recv_sem=pass_recv.at[at],
            device_id=other,
            device_id_type=pl.DeviceIdType.MESH,
        )

    def forwarded(stage):
        return pltpu.make_async_remote_copy(
            src_ref=traces.at[stage],
            dst_ref=traces.at[TSTEPS + stage],
            send_sem=pass_send.at[3 + stage],
            recv_sem=pass_recv.at[3 + stage],
            device_id=other,
            device_id_type=pl.DeviceIdType.MESH,
        )

    def greet(offset, carry):
        pl.semaphore_signal(
            barrier, inc=1, device_id=peer(offset), device_id_type=pl.DeviceIdType.MESH
        )
        return carry

    pl.semaphore_signal(barrier, inc=1, device_id=other, device_id_type=pl.DeviceIdType.MESH)
    lax.fori_loop(1, tiles, greet, 0)
    tables = [
        pltpu.make_async_copy(ref, kept, table_sem.at[at])
        for at, (ref, kept) in enumerate(zip(indices, held))
    ]
    loads = [
        pltpu.make_async_copy(ref, states.at[0, pl.ds(base, count), :], load_sem.at[at])
        for at, (ref, base, count) in enumerate(parts)
    ]
    loads.append(pltpu.make_async_copy(fields[3], older, load_sem.at[3]))
    loads.append(pltpu.make_async_copy(fields[4], old, load_sem.at[4]))
    for load in tables + loads:
        load.start()
    pl.semaphore_wait(barrier, tiles)

    @pl.when(base_level)
    def _():
        for at in range(3):
            handed(at).start()

    for load in tables:
        load.wait()
    fill_tables(peers, matches, slots, partner, inner, send, place)
    for stage in range(TSTEPS):
        traces[stage, me] = jnp.zeros(traces.shape[2:], jnp.float32)
    for load in loads:
        load.wait()

    def arrive(stage):
        def finish(offset, carry):
            swap(stage, offset).wait()
            return carry

        lax.fori_loop(1, tiles, finish, 0)

    def sweep(work):
        rows = SIZE // 20

        def chunk(at, carry):
            work(pl.ds(pl.multiple_of(at * rows, rows), rows))
            return carry

        lax.fori_loop(0, 20, chunk, 0)

    def step(t, carry):
        def on(base, at):
            return pl.when((level == 0) & (t == at) if base else (level > 0) & (t == at))

        state, rate = states.at[t], rates.at[t]
        stage = jnp.where(t <= 1, t, 2)
        leaving = jnp.where(base_level, t <= 2, (t <= 1) | (t == 4))
        lasting = jnp.where(base_level, t <= 2, (t != 1) & (t != 4))

        @on(False, 2)
        def _():
            for at in range(3):
                handed(at).wait_recv()

        @pl.when(leaving | lasting)
        def _():
            spread_traces(state, spread)

        @pl.when(leaving)
        def _():
            leave = lax.dot_general(
                send[...], spread[...], (((1,), (1,)), ((), ())), preferred_element_type=jnp.float32
            )
            leave = leave[:, :ROWS] + leave[:, ROWS:]
            buffer[stage] = leave.reshape(tiles, FCAP, ROWS)

            def begin(offset, carry):
                swap(stage, offset).start()
                return carry

            lax.fori_loop(1, tiles, begin, 0)

        @pl.when(lasting)
        def _():
            planes_and_views(state, spread, inner, flow, high, low, rate, view)
            remaining_volume(flow, high, low, blocks, rate)

            @pl.when(base_level | (t == 0))
            def _():
                arrive(stage)

            @on(True, 0)
            def _():
                forwarded(0).start()

            @on(True, 2)
            def _():
                for at in range(3):
                    handed(at).wait_send()
                forwarded(1).start()
                forwarded(2).start()

            @on(False, 2)
            def _():
                forwarded(0).wait_recv()

            @on(False, 3)
            def _():
                arrive(1)
                forwarded(1).wait_recv()

            @on(False, 6)
            def _():
                forwarded(2).wait_recv()

            @on(False, 7)
            def _():
                arrive(2)

            own = jnp.where(
                base_level | (t == 0),
                t,
                jnp.where(t == 3, 1, jnp.where(t == 7, 2, jnp.where(t == 2, 3, t - 1))),
            )
            mixed = (level > 0) & ((t == 3) | (t == 7))
            newer = jnp.where(mixed, jnp.where(t == 3, 4, 5), own)
            elder = jnp.where(mixed, newer - 1, own)
            share = jnp.where(mixed, weight_next, 0.0)
            seen = traces[own] + share * (traces[newer] - traces[elder])
            lift_all(state, view, seen.reshape(tiles * FCAP, ROWS), place, orient, rate)

        @pl.when(t == 0)
        def _():
            def work(rows):
                extra = weight_back * older[rows, :] + (weight_here - 1.0) * old[rows, :]
                states[1, rows, :] = states[0, rows, :] + step_size * (
                    rates[0, rows, :] + upper * extra
                )

            sweep(work)

        @on(True, 1)
        def _():
            def work(rows):
                states[2, rows, :] = states[1, rows, :] + step_size * rates[1, rows, :]

            sweep(work)

        @on(True, 2)
        def _():
            def work(rows):
                moved = states[2, rows, :] + step_size * rates[2, rows, :] - states[0, rows, :]
                out[rows, :] = moved * SCALE

            sweep(work)

        @on(False, 2)
        def _():
            def work(rows):
                below = step_size * rates[2, rows, :]
                states[3, rows, :] = states[1, rows, :] + weight_next * below
                states[5, rows, :] = states[2, rows, :] + below

            sweep(work)

        @on(False, 3)
        def _():
            def work(rows):
                states[4, rows, :] = states[3, rows, :] + step_size * (
                    rates[3, rows, :]
                    + weight_back * old[rows, :]
                    + (weight_here - 1.0) * rates[2, rows, :]
                )

            sweep(work)

        @on(False, 5)
        def _():
            def work(rows):
                below = step_size * rates[5, rows, :]
                states[7, rows, :] = states[4, rows, :] + weight_next * below
                states[6, rows, :] = states[5, rows, :] + below

            sweep(work)

        @on(False, 7)
        def _():
            def work(rows):
                change = (
                    rates[7, rows, :]
                    + weight_back * rates[2, rows, :]
                    + (weight_here - 1.0) * rates[5, rows, :]
                    + weight_next * rates[6, rows, :]
                )
                moved = states[7, rows, :] + step_size * change - states[0, rows, :]
                out[rows, :] = moved * SCALE

            sweep(work)

        return carry

    lax.fori_loop(0, STEPS, step, 0)

    @pl.when(base_level)
    def _():
        for stage in range(TSTEPS):
            forwarded(stage).wait_send()


def window_of(fields, indices):
    tiles = lax.axis_size("tile")
    width = fields[0].shape[1]
    faces = indices[3].shape[1]
    full = (SIZE, width)
    f32, bf16 = jnp.float32, jnp.bfloat16
    operands = [*fields, *indices, jnp.asarray(block_numbers())]
    return pl.pallas_call(
        window_kernel,
        out_shape=jax.ShapeDtypeStruct(full, f32),
        in_specs=[pl.BlockSpec(memory_space=pl.ANY)] * len(operands),
        out_specs=VMEM,
        scratch_shapes=[
            pltpu.VMEM((STEPS,) + full, f32),
            pltpu.VMEM((STEPS,) + full, f32),
            pltpu.VMEM(full, f32),
            pltpu.VMEM(full, f32),
            *[pltpu.VMEM(x.shape, x.dtype) for x in operands[5:]],
            pltpu.VMEM((faces, faces), bf16),
            pltpu.VMEM((tiles * FCAP, faces), bf16),
            pltpu.VMEM((tiles * FCAP, faces), bf16),
            pltpu.VMEM((2 * ROWS, faces), bf16),
            pltpu.VMEM(full, f32),
            pltpu.VMEM(full, bf16),
            pltpu.VMEM(full, bf16),
            pltpu.VMEM((6 * ROWS, width), f32),
            pltpu.VMEM((TSTEPS, tiles, FCAP, ROWS), f32),
            pltpu.VMEM((2 * TSTEPS, tiles, FCAP, ROWS), f32),
            pltpu.SemaphoreType.DMA((TSTEPS, tiles)),
            pltpu.SemaphoreType.DMA((TSTEPS, tiles)),
            pltpu.SemaphoreType.DMA((5,)),
            pltpu.SemaphoreType.DMA((6,)),
            pltpu.SemaphoreType.DMA((6,)),
            pltpu.SemaphoreType.DMA((6,)),
        ],
        compiler_params=pltpu.CompilerParams(
            collective_id=2, has_side_effects=True, vmem_limit_bytes=56 << 20
        ),
    )(*operands)


def turning():
    nodes = np.arange(NODES)
    blocks = []
    for orient in range(4):
        source = nodes.reshape(NP, NP)
        if orient >= 2:
            source = source[::-1, ::-1]
        if orient % 2 == 1:
            source = source.T
        block = np.zeros((NODES, NODES), np.float32)
        block[nodes, source.reshape(-1)] = 1.0
        blocks.append(block)
    return np.concatenate(blocks, axis=1)


def body(
    density,
    momentum,
    energy,
    rhs_older,
    rhs_old,
    peer_tile,
    peer_index,
    boundary_slot,
    face_partner,
    face_orient,
):
    width = density.shape[-1]
    if lax.axis_size("level") == 2:
        fields = [density, momentum, energy, rhs_older, rhs_old]
        indices = [peer_tile, peer_index, boundary_slot, face_partner, face_orient]
        result = window_of([field.reshape(-1, width) for field in fields], indices)
        return result.reshape(rhs_old.shape)
    start = jnp.concatenate(
        [
            density.reshape(-1, width),
            momentum.reshape(-1, width),
            energy.reshape(-1, width),
        ],
        axis=0,
    )
    level = lax.axis_index("level")
    tiles = lax.axis_size("tile")
    peers = peer_tile[0]
    matches = peer_index[0]
    slots = boundary_slot[0]
    partner = face_partner[0]
    orient = face_orient[0]
    count = peers.shape[0]
    faces = partner.shape[0]
    same_peer = peers[:, None] == peers[None, :]
    listing = jnp.arange(count, dtype=jnp.int32)
    send_rank = jnp.sum(same_peer & (matches[None, :] < matches[:, None]), axis=1, dtype=jnp.int32)
    recv_rank = jnp.sum(same_peer & (listing[None, :] < listing[:, None]), axis=1, dtype=jnp.int32)
    places = jnp.arange(tiles * FCAP, dtype=jnp.int32)
    ids = jnp.arange(faces, dtype=jnp.int32)
    exact = jnp.bfloat16
    at_slot = (slots[:, None] == ids[None, :]).astype(exact)

    def routing(rank):
        onehot = (places[:, None] == (peers * FCAP + rank)[None, :]).astype(exact)
        return jnp.dot(onehot, at_slot, preferred_element_type=jnp.float32).astype(exact)

    send = routing(send_rank)
    place = routing(recv_rank)
    inner = ((ids[:, None] == partner[None, :]) & (partner != ids)[None, :]).astype(exact)
    masks = (orient[None, :] == jnp.arange(8, dtype=jnp.int32)[:, None]).astype(jnp.float32)
    turn = jnp.asarray(turning(), exact)
    numbers = derivative_numbers()
    diagonals = np.stack(
        [
            np.stack([-metric * numbers[k, (k + shift) % NP] for k in range(NP)])
            for shift in range(NP)
        ]
    ).astype(np.float32)
    rolled = jnp.broadcast_to(jnp.asarray(diagonals)[:, :, None], (NP, NP, width))

    tables = (masks, turn, inner, send, place, rolled)

    def rates(states):
        return rates_of(states, tables)

    older = rhs_older.reshape(-1, width)
    old = rhs_old.reshape(-1, width)

    def advance(state, own_rate, older, old, below):
        corrected = (
            state
            + step_size * (own_rate - old)
            + step_size * (weight_back * older + weight_here * old + weight_next * below)
        )
        return jnp.where(level == 0, state + step_size * own_rate, corrected)

    state = start
    for repeat in range(TSTEPS):
        own_rate = rates([state])[0]
        below = shifted(own_rate, "level", 1)
        state = advance(state, own_rate, older, old, below)
        older = old
        old = below
    return ((state - start) / (TSTEPS * step_size)).reshape(rhs_old.shape)


def solution(mesh):
    return jax.shard_map(
        body,
        mesh=mesh,
        in_specs=(
            P("level", None, None, None, "tile"),
            P("level", None, None, None, None, "tile"),
            P("level", None, None, None, "tile"),
            P("level", None, None, None, None, "tile"),
            P("level", None, None, None, None, "tile"),
            P("tile", None),
            P("tile", None),
            P("tile", None),
            P("tile", None),
            P("tile", None),
        ),
        out_specs=P("level", None, None, None, None, "tile"),
        check_vma=False,
    )
```

```python
import functools

import jax
import jax.numpy as jnp
import numpy as np
from jax import lax
from jax.experimental import pallas as pl
from jax.experimental.pallas import tpu as pltpu
from jax.sharding import PartitionSpec as P

NP = 8
TSTEPS = 3
FCAP = 8


step_size = 0.02
penalty = 2.5
metric = 0.1
lift_factor = 2.8
weight_back = -1.0 / 12.0
weight_here = 8.0 / 12.0
weight_next = 5.0 / 12.0


def shifted(block, axis, distance):
    devices = range(lax.axis_size(axis))
    route = [(i - distance, i) for i in devices if i - distance in devices]
    return lax.ppermute(block, axis, route)


def lobatto_points():
    degree = NP - 1
    points = np.cos(np.pi * np.arange(degree + 1) / degree)
    table = np.zeros((degree + 1, degree + 1))
    for sweep in range(60):
        table[:, 0] = 1.0
        table[:, 1] = points
        for order in range(2, degree + 1):
            table[:, order] = (
                (2 * order - 1) * points * table[:, order - 1] - (order - 1) * table[:, order - 2]
            ) / order
        points = points - (points * table[:, degree] - table[:, degree - 1]) / (
            (degree + 1) * table[:, degree]
        )
    table[:, 0] = 1.0
    table[:, 1] = points
    for order in range(2, degree + 1):
        table[:, order] = (
            (2 * order - 1) * points * table[:, order - 1] - (order - 1) * table[:, order - 2]
        ) / order
    return (points[::-1], table[::-1, degree])


def derivative_numbers():
    degree = NP - 1
    points, values = lobatto_points()
    identity = np.eye(NP)
    spread = points[:, None] - points[None, :] + identity
    table = values[:, None] / values[None, :] / spread
    table = table * (1.0 - identity)
    table[0, 0] = -degree * (degree + 1) / 4.0
    table[degree, degree] = degree * (degree + 1) / 4.0
    return np.asarray(table, dtype=np.float32)

NV = 5
NODES = NP * NP
ROWS = NV * NODES
SIZE = NV * NP * NODES
CELLS = NP * NODES
STEPS = 8
SCALE = 1.0 / (TSTEPS * step_size)


def primitive(w):
    inverse = 1.0 / w[0]
    velocity = [w[c] * inverse for c in (1, 2, 3)]
    pressure = 0.4 * (w[4] - 0.5 * (w[1] * velocity[0] + w[2] * velocity[1] + w[3] * velocity[2]))
    return velocity, pressure


def flux(w, velocity, pressure, direction):
    carried = w[1 + direction]
    parts = [carried]
    for column in range(3):
        product = carried * velocity[column]
        if column == direction:
            product = product + pressure
        parts.append(product)
    parts.append((w[4] + pressure) * velocity[direction])
    return parts


def pieces_of(x):
    high = x.astype(jnp.bfloat16)
    rest = x - high.astype(jnp.float32)
    middle = rest.astype(jnp.bfloat16)
    low = (rest - middle.astype(jnp.float32)).astype(jnp.bfloat16)
    return [high, middle, low]


def face_rows(which):
    direction, end = which // 2, (NP - 1) * (which % 2)
    return direction, end


def trace_rows(ref, which, v):
    direction, end = face_rows(which)
    base = v * NP * NODES
    if direction == 0:
        return ref[pl.ds(base + end * NODES, NODES), :]
    if direction == 1:
        return jnp.concatenate(
            [ref[pl.ds(base + i * NODES + end * NP, NP), :] for i in range(NP)], axis=0
        )
    return ref[pl.ds(base + end, NODES, stride=NP), :]


def gather_traces(state, masks, turn, turned):
    width = state.shape[1]
    for which in range(6):
        lanes = pl.ds(which * width, width)
        mask = [jnp.broadcast_to(masks[o : o + 1, lanes], (NODES, width)) for o in range(4)]
        for v in range(NV):
            for at, piece in enumerate(pieces_of(trace_rows(state, which, v))):
                wide = piece.astype(jnp.float32)
                stacked = jnp.concatenate([(wide * m).astype(jnp.bfloat16) for m in mask], axis=0)
                out = jnp.dot(turn[...], stacked, preferred_element_type=jnp.float32)
                turned[at, pl.ds(v * NODES, NODES), lanes] = out.astype(jnp.bfloat16)


def outgoing_of(turned, send):
    outgoing = None
    for at in range(3):
        leave = lax.dot_general(
            send[...], turned[at], (((1,), (1,)), ((), ())), preferred_element_type=jnp.float32
        )
        outgoing = leave if outgoing is None else outgoing + leave
    return outgoing


def inner_of(turned, inner):
    total = None
    for at in range(3):
        part = jnp.dot(turned[at], inner[...], preferred_element_type=jnp.float32)
        total = part if total is None else total + part
    return total


def outer_of(arrived, place):
    total = None
    for piece in pieces_of(arrived):
        part = lax.dot_general(
            piece, place[...], (((0,), (0,)), ((), ())), preferred_element_type=jnp.float32
        )
        total = part if total is None else total + part
    return total


def volume_of(state, rolled, rate):
    numbers = derivative_numbers()

    def derived(fields):
        even = [fields[index] + fields[NP - 1 - index] for index in range(NP // 2)]
        odd = [fields[index] - fields[NP - 1 - index] for index in range(NP // 2)]
        results = [None] * NP
        for target in range(NP // 2):
            near = None
            far = None
            for index in range(NP // 2):
                here = float(numbers[target, index])
                there = float(numbers[target, NP - 1 - index])
                one = (-0.5 * metric * (here + there)) * even[index]
                two = (-0.5 * metric * (here - there)) * odd[index]
                near = one if near is None else near + one
                far = two if far is None else far + two
            results[target] = far + near
            results[NP - 1 - target] = far - near
        return results

    def at(v, i, j):
        return pl.ds(pl.multiple_of(v * NP * NODES + i * NODES + j * NP, NP), NP)

    def along_first(j, carry):
        across = [[None] * NP for v in range(NV)]
        down = [[None] * NP for v in range(NV)]
        for i in range(NP):
            w = [state[at(v, i, j), :] for v in range(NV)]
            velocity, pressure = primitive(w)
            for v, part in enumerate(flux(w, velocity, pressure, 0)):
                across[v][i] = part
            for v, part in enumerate(flux(w, velocity, pressure, 2)):
                total = rolled[0] * part
                for shift in range(1, NP):
                    total = total + rolled[shift] * pltpu.roll(part, NP - shift, 0)
                down[v][i] = total
        for v in range(NV):
            for i, part in enumerate(derived(across[v])):
                rate[at(v, i, j), :] = part + down[v][i]
        return carry

    def along_second(i, carry):
        across = [[None] * NP for v in range(NV)]
        for j in range(NP):
            w = [state[at(v, i, j), :] for v in range(NV)]
            velocity, pressure = primitive(w)
            for v, part in enumerate(flux(w, velocity, pressure, 1)):
                across[v][j] = part
        for v in range(NV):
            for j, part in enumerate(derived(across[v])):
                rate[at(v, i, j), :] = rate[at(v, i, j), :] + part
        return carry

    lax.fori_loop(0, NP, along_first, 0)
    lax.fori_loop(0, NP, along_second, 0)


def lift_faces(state, view, rate):
    width = state.shape[1]
    for which in range(6):
        direction, end = face_rows(which)
        normal = 2.0 * (which % 2) - 1.0
        lanes = pl.ds(which * width, width)

        def lift(row, carry):
            def rows(v):
                base = v * NP * NODES
                if direction == 0:
                    return pl.ds(pl.multiple_of(base + end * NODES + row * NP, NP), NP)
                if direction == 1:
                    return pl.ds(pl.multiple_of(base + row * NODES + end * NP, NP), NP)
                return pl.ds(base + row * NODES + end, NP, stride=NP)

            own = [state[rows(v), :] for v in range(NV)]
            far = [
                view[pl.ds(pl.multiple_of(v * NODES + row * NP, NP), NP), lanes]
                for v in range(NV)
            ]
            own_flux = flux(own, *primitive(own), direction)
            far_flux = flux(far, *primitive(far), direction)
            for v in range(NV):
                jump = (0.5 * normal) * (far_flux[v] - own_flux[v]) - (0.5 * penalty) * (
                    far[v] - own[v]
                )
                rate[rows(v), :] = rate[rows(v), :] - lift_factor * jump
            return carry

        lax.fori_loop(0, NP, lift, 0)


VMEM = pl.BlockSpec(memory_space=pltpu.VMEM)


def rate_kernel(count, *refs):
    states, refs = refs[:count], refs[count:]
    masks, turn, inner, send, place, rolled = refs[:6]
    rates, refs = refs[6 : 6 + count], refs[6 + count :]
    turned, views, buffer, landed, send_sem, recv_sem = refs
    tiles = lax.axis_size("tile")
    me = lax.axis_index("tile")
    barrier = pltpu.get_barrier_semaphore()

    def peer(offset):
        return {"tile": lax.rem(me + offset, tiles)}

    def copy(offset):
        return pltpu.make_async_remote_copy(
            src_ref=buffer.at[lax.rem(me + offset, tiles)],
            dst_ref=landed.at[me],
            send_sem=send_sem.at[offset],
            recv_sem=recv_sem.at[offset],
            device_id=peer(offset),
            device_id_type=pl.DeviceIdType.MESH,
        )

    def greet(offset, carry):
        pl.semaphore_signal(
            barrier, inc=1, device_id=peer(offset), device_id_type=pl.DeviceIdType.MESH
        )
        return carry

    def begin(offset, carry):
        copy(offset).start()
        return carry

    def finish(offset, carry):
        copy(offset).wait()
        return carry

    lax.fori_loop(1, tiles, greet, 0)
    for at in range(count):
        gather_traces(states[at], masks, turn, turned.at[at])
        leave = outgoing_of(turned.at[at], send)
        buffer[:, at * FCAP : (at + 1) * FCAP, :] = leave.reshape(tiles, FCAP, ROWS)
    pl.semaphore_wait(barrier, tiles - 1)
    lax.fori_loop(1, tiles, begin, 0)
    landed[me] = jnp.zeros(landed.shape[1:], jnp.float32)
    for at in range(count):
        views[at] = inner_of(turned.at[at], inner)
        volume_of(states[at], rolled, rates[at])
    lax.fori_loop(1, tiles, finish, 0)
    for at in range(count):
        arrived = landed[:, at * FCAP : (at + 1) * FCAP, :].reshape(tiles * FCAP, ROWS)
        views[at] = views[at] + outer_of(arrived, place)
        lift_faces(states[at], views.at[at], rates[at])


def rates_of(states, tables):
    tiles = lax.axis_size("tile")
    count = len(states)
    slots = tables[0].shape[1]
    like = jax.ShapeDtypeStruct(states[0].shape, jnp.float32)
    return pl.pallas_call(
        functools.partial(rate_kernel, count),
        out_shape=[like] * count,
        in_specs=[VMEM] * (count + len(tables)),
        out_specs=[VMEM] * count,
        scratch_shapes=[
            pltpu.VMEM((count, 3, ROWS, slots), jnp.bfloat16),
            pltpu.VMEM((count, ROWS, slots), jnp.float32),
            pltpu.VMEM((tiles, count * FCAP, ROWS), jnp.float32),
            pltpu.VMEM((tiles, count * FCAP, ROWS), jnp.float32),
            pltpu.SemaphoreType.DMA((tiles,)),
            pltpu.SemaphoreType.DMA((tiles,)),
        ],
        compiler_params=pltpu.CompilerParams(
            collective_id=count - 1, has_side_effects=True, vmem_limit_bytes=40 << 20
        ),
    )(*states, *tables)


def pieces_pair(x):
    high = x.astype(jnp.bfloat16)
    return high, (x - high.astype(jnp.float32)).astype(jnp.bfloat16)


def fluxes(w):
    inverse = 1.0 / w[0]
    velocity = [w[c] * inverse for c in (1, 2, 3)]
    product = {}
    for a in range(3):
        for b in range(a, 3):
            product[a, b] = product[b, a] = w[1 + a] * velocity[b]
    pressure = 0.4 * (w[4] - 0.5 * (product[0, 0] + product[1, 1] + product[2, 2]))
    total = w[4] + pressure
    return [
        [w[1 + d]]
        + [product[d, c] + pressure if c == d else product[d, c] for c in range(3)]
        + [total * velocity[d]]
        for d in range(3)
    ]


def derived(fields):
    numbers = derivative_numbers()
    even = [fields[index] + fields[NP - 1 - index] for index in range(NP // 2)]
    odd = [fields[index] - fields[NP - 1 - index] for index in range(NP // 2)]
    results = [None] * NP
    for target in range(NP // 2):
        near = None
        far = None
        for index in range(NP // 2):
            here = float(numbers[target, index])
            there = float(numbers[target, NP - 1 - index])
            one = (-0.5 * metric * (here + there)) * even[index]
            two = (-0.5 * metric * (here - there)) * odd[index]
            near = one if near is None else near + one
            far = two if far is None else far + two
        results[target] = far + near
        results[NP - 1 - target] = far - near
    return results


HALF = NP * NODES // 2


def block_numbers():
    whole = np.kron(np.eye(HALF // NP), -metric * derivative_numbers()).astype(np.float32)
    high = whole.astype(jnp.bfloat16)
    low = (whole - high.astype(np.float32)).astype(jnp.bfloat16)
    return np.concatenate([high, low, high], axis=1)


def spread_traces(state, spread):
    width = state.shape[1]
    for which in range(6):
        lanes = pl.ds(which * width, width)
        for v in range(NV):
            high, low = pieces_pair(trace_rows(state, which, v))
            spread[pl.ds(v * NODES, NODES), lanes] = high
            spread[pl.ds(ROWS + v * NODES, NODES), lanes] = low


def node_rows(v, i, j, count=NP):
    return pl.ds(v * NP * NODES + i * NODES + j * NP, count)


def planes_and_views(state, spread, inner, flow, high, low, rate, view):
    width = state.shape[1]
    for i in range(NP):
        across = [[None] * NP for v in range(NV)]
        for j in range(0, NP, 2):
            thirds = [None, None]
            for half in range(2):
                w = [state[node_rows(v, i, j + half), :] for v in range(NV)]
                one, two, thirds[half] = fluxes(w)
                for v in range(NV):
                    across[v][j + half] = two[v]
                    flow[node_rows(v, i, j + half), :] = one[v]
            for v in range(NV):
                both = jnp.concatenate([thirds[0][v], thirds[1][v]], axis=0)
                upper, lower = pieces_pair(both)
                high[node_rows(v, i, j, 2 * NP), :] = upper
                low[node_rows(v, i, j, 2 * NP), :] = lower
        for v in range(NV):
            for j, part in enumerate(derived(across[v])):
                rate[node_rows(v, i, j), :] = part
        if i % 2 == 0 and i < 6:
            both = jnp.dot(
                spread[...], inner[:, i * width : (i + 2) * width],
                preferred_element_type=jnp.float32,
            )
            both = both[:ROWS] + both[ROWS:]
            for half in range(2):
                view[pl.ds((i + half) * ROWS, ROWS), :] = both[:, half * width : (half + 1) * width]


def remaining_volume(flow, high, low, blocks, rate):
    width = flow.shape[1]
    for v in range(NV):
        base = v * NP * NODES

        def pair(ref):
            return jnp.concatenate(
                [ref[pl.ds(base, HALF), :], ref[pl.ds(base + HALF, HALF), :]], axis=1
            )

        upper, lower = pair(high), pair(low)
        down = jnp.dot(
            blocks[...],
            jnp.concatenate([upper, upper, lower], axis=0),
            preferred_element_type=jnp.float32,
        )
        for j in range(NP):
            parts = derived([flow[node_rows(v, i, j), :] for i in range(NP)])
            for i, part in enumerate(parts):
                row, lane = (i % 4) * NODES + j * NP, (i // 4) * width
                rows = node_rows(v, i, j)
                rate[rows, :] = rate[rows, :] + part + down[row : row + NP, lane : lane + width]


def lift_all(state, view, traces, place, orient, rate):
    width = state.shape[1]
    upper, lower = pieces_pair(traces.T)
    sides = jnp.concatenate([upper, lower], axis=0)
    ahead = lax.broadcasted_iota(jnp.int32, (NP, width), 0)
    for which in range(6):
        direction, end = face_rows(which)
        normal = 2.0 * (which % 2) - 1.0
        lanes = pl.ds(which * width, width)
        if which % 2 == 0:
            outer = jnp.dot(
                sides, place[:, which * width : (which + 2) * width],
                preferred_element_type=jnp.float32,
            )
            outer = outer[:ROWS] + outer[ROWS:]
            for half in range(2):
                rows = pl.ds((which + half) * ROWS, ROWS)
                view[rows, :] = view[rows, :] + outer[:, half * width : (half + 1) * width]
        orients = jnp.broadcast_to(orient[0:1, lanes], (NP, width))
        crossed = (orients & 1) == 1
        turned = orients >= 2
        order = jnp.where(turned, NP - 1 - ahead, ahead)

        def rows_of(v, row):
            base = v * NP * NODES
            if direction == 0:
                return pl.ds(base + end * NODES + row * NP, NP)
            if direction == 1:
                return pl.ds(base + row * NODES + end * NP, NP)
            return pl.ds(base + row * NODES + end, NP, stride=NP)

        for near in range(NP // 2):
            pair = [near, NP - 1 - near]
            far = [[], []]
            for v in range(NV):
                base = which * ROWS + v * NODES
                seen = [
                    jnp.where(
                        crossed,
                        view[pl.ds(base + row, NP, stride=NP), :],
                        view[pl.ds(base + row * NP, NP), :],
                    )
                    for row in pair
                ]
                for half in range(2):
                    picked = jnp.where(turned, seen[1 - half], seen[half])
                    far[half].append(
                        jnp.take_along_axis(picked, order, axis=0, mode="promise_in_bounds")
                    )
            for half in range(2):
                rows = [rows_of(v, pair[half]) for v in range(NV)]
                own = [state[rows[v], :] for v in range(NV)]
                own_flux = flux(own, *primitive(own), direction)
                far_flux = flux(far[half], *primitive(far[half]), direction)
                for v in range(NV):
                    jump = (0.5 * normal) * (far_flux[v] - own_flux[v]) - (0.5 * penalty) * (
                        far[half][v] - own[v]
                    )
                    rate[rows[v], :] = rate[rows[v], :] - lift_factor * jump


def table_rows(ref, fill):
    row = ref[...].astype(jnp.float32)
    extra = -row.shape[1] % 128
    if extra > 0:
        row = jnp.concatenate([row, jnp.full((1, extra), fill, jnp.float32)], axis=1)
    return row


def fill_tables(peers, matches, slots, partner, inner, send, place):
    faces = partner.shape[1]
    pack = 16

    def some(at, carry):
        base = pl.multiple_of(at * pack, pack)
        ids = lax.broadcasted_iota(jnp.int32, (pack, faces), 0) + base
        lane = lax.broadcasted_iota(jnp.int32, (pack, faces), 1)
        mate = jnp.broadcast_to(partner[...], (pack, faces))
        hit = jnp.where((ids == mate) & (mate != lane), 1.0, 0.0)
        inner[pl.ds(base, pack), :] = hit.astype(jnp.bfloat16)
        return carry

    lax.fori_loop(0, faces // pack, some, 0)
    peer = table_rows(peers, -1.0)
    match = table_rows(matches, -1.0)
    slot = table_rows(slots, -1.0)
    count = peer.shape[1]
    square = (count, count)
    peer_across = jnp.broadcast_to(peer, square)
    match_across = jnp.broadcast_to(match, square)
    same = peer_across.T == peer_across
    lower = match_across.T < match_across
    sooner = lax.broadcasted_iota(jnp.int32, square, 0) < lax.broadcasted_iota(jnp.int32, square, 1)
    slot_of = lax.broadcasted_iota(jnp.int32, (faces, count), 0).astype(jnp.float32)
    at_slot = jnp.where(slot_of == jnp.broadcast_to(slot, (faces, count)), 1.0, 0.0)
    at_slot = at_slot.astype(jnp.bfloat16)
    places = send.shape[0]
    spots = lax.broadcasted_iota(jnp.int32, (places, count), 0).astype(jnp.float32)
    for ahead, table in ((lower, send), (sooner, place)):
        rank = jnp.sum(jnp.where(same & ahead, 1.0, 0.0), axis=0, keepdims=True)
        spot = jnp.broadcast_to(peer * FCAP + rank, (places, count))
        onehot = jnp.where(spots == spot, 1.0, 0.0).astype(jnp.bfloat16)
        routed = lax.dot_general(
            onehot, at_slot, (((1,), (1,)), ((), ())), preferred_element_type=jnp.float32
        )
        table[...] = routed.astype(jnp.bfloat16)


def window_kernel(*refs):
    fields, refs = refs[:5], refs[5:]
    indices, refs = refs[:6], refs[6:]
    out, refs = refs[0], refs[1:]
    states, rates, older, old, refs = refs[0], refs[1], refs[2], refs[3], refs[4:]
    held, refs = refs[:6], refs[6:]
    inner, send, place, spread, flow, high, low, view, refs = *refs[:8], refs[8:]
    buffer, traces, send_sem, recv_sem, load_sem, table_sem, pass_send, pass_recv = refs
    peers, matches, slots, partner, orient, blocks = held
    tiles = lax.axis_size("tile")
    me = lax.axis_index("tile")
    level = lax.axis_index("level")
    base_level = level == 0
    upper = (level > 0).astype(jnp.float32)
    other = {"level": 1 - level}
    barrier = pltpu.get_barrier_semaphore()
    parts = [
        (fields[0], 0, CELLS),
        (fields[1], CELLS, 3 * CELLS),
        (fields[2], 4 * CELLS, CELLS),
    ]

    def peer(offset):
        return {"tile": lax.rem(me + offset, tiles)}

    def swap(stage, offset):
        return pltpu.make_async_remote_copy(
            src_ref=buffer.at[stage, lax.rem(me + offset, tiles)],
            dst_ref=traces.at[stage, me],
            send_sem=send_sem.at[stage, offset],
            recv_sem=recv_sem.at[stage, offset],
            device_id=peer(offset),
            device_id_type=pl.DeviceIdType.MESH,
        )

    def handed(at):
        ref, base, count = parts[at]
        return pltpu.make_async_remote_copy(
            src_ref=ref,
            dst_ref=states.at[2, pl.ds(base, count), :],
            send_sem=pass_send.at[at],
            recv_sem=pass_recv.at[at],
            device_id=other,
            device_id_type=pl.DeviceIdType.MESH,
        )

    def forwarded(stage):
        return pltpu.make_async_remote_copy(
            src_ref=traces.at[stage],
            dst_ref=traces.at[TSTEPS + stage],
            send_sem=pass_send.at[3 + stage],
            recv_sem=pass_recv.at[3 + stage],
            device_id=other,
            device_id_type=pl.DeviceIdType.MESH,
        )

    def greet(offset, carry):
        pl.semaphore_signal(
            barrier, inc=1, device_id=peer(offset), device_id_type=pl.DeviceIdType.MESH
        )
        return carry

    pl.semaphore_signal(barrier, inc=1, device_id=other, device_id_type=pl.DeviceIdType.MESH)
    lax.fori_loop(1, tiles, greet, 0)
    tables = [
        pltpu.make_async_copy(ref, kept, table_sem.at[at])
        for at, (ref, kept) in enumerate(zip(indices, held))
    ]
    loads = [
        pltpu.make_async_copy(ref, states.at[0, pl.ds(base, count), :], load_sem.at[at])
        for at, (ref, base, count) in enumerate(parts)
    ]
    loads.append(pltpu.make_async_copy(fields[3], older, load_sem.at[3]))
    loads.append(pltpu.make_async_copy(fields[4], old, load_sem.at[4]))
    for load in tables + loads:
        load.start()
    pl.semaphore_wait(barrier, tiles)

    @pl.when(base_level)
    def _():
        for at in range(3):
            handed(at).start()

    for load in tables:
        load.wait()
    fill_tables(peers, matches, slots, partner, inner, send, place)
    for stage in range(TSTEPS):
        traces[stage, me] = jnp.zeros(traces.shape[2:], jnp.float32)
    for load in loads:
        load.wait()

    def arrive(stage):
        def finish(offset, carry):
            swap(stage, offset).wait()
            return carry

        lax.fori_loop(1, tiles, finish, 0)

    def sweep(work):
        rows = SIZE // 20

        def chunk(at, carry):
            work(pl.ds(pl.multiple_of(at * rows, rows), rows))
            return carry

        lax.fori_loop(0, 20, chunk, 0)

    def step(t, carry):
        def on(base, at):
            return pl.when((level == 0) & (t == at) if base else (level > 0) & (t == at))

        state, rate = states.at[t], rates.at[t]
        stage = jnp.where(t <= 1, t, 2)
        leaving = jnp.where(base_level, t <= 2, (t <= 1) | (t == 4))
        lasting = jnp.where(base_level, t <= 2, (t != 1) & (t != 4))

        @on(False, 2)
        def _():
            for at in range(3):
                handed(at).wait_recv()

        @pl.when(leaving | lasting)
        def _():
            spread_traces(state, spread)

        @pl.when(leaving)
        def _():
            leave = lax.dot_general(
                send[...], spread[...], (((1,), (1,)), ((), ())), preferred_element_type=jnp.float32
            )
            leave = leave[:, :ROWS] + leave[:, ROWS:]
            buffer[stage] = leave.reshape(tiles, FCAP, ROWS)

            def begin(offset, carry):
                swap(stage, offset).start()
                return carry

            lax.fori_loop(1, tiles, begin, 0)

        @pl.when(lasting)
        def _():
            planes_and_views(state, spread, inner, flow, high, low, rate, view)
            remaining_volume(flow, high, low, blocks, rate)

            @pl.when(base_level | (t == 0))
            def _():
                arrive(stage)

            @on(True, 0)
            def _():
                forwarded(0).start()

            @on(True, 2)
            def _():
                for at in range(3):
                    handed(at).wait_send()
                forwarded(1).start()
                forwarded(2).start()

            @on(False, 2)
            def _():
                forwarded(0).wait_recv()

            @on(False, 3)
            def _():
                arrive(1)
                forwarded(1).wait_recv()

            @on(False, 6)
            def _():
                forwarded(2).wait_recv()

            @on(False, 7)
            def _():
                arrive(2)

            own = jnp.where(
                base_level | (t == 0),
                t,
                jnp.where(t == 3, 1, jnp.where(t == 7, 2, jnp.where(t == 2, 3, t - 1))),
            )
            mixed = (level > 0) & ((t == 3) | (t == 7))
            newer = jnp.where(mixed, jnp.where(t == 3, 4, 5), own)
            elder = jnp.where(mixed, newer - 1, own)
            share = jnp.where(mixed, weight_next, 0.0)
            seen = traces[own] + share * (traces[newer] - traces[elder])
            lift_all(state, view, seen.reshape(tiles * FCAP, ROWS), place, orient, rate)

        @pl.when(t == 0)
        def _():
            def work(rows):
                extra = weight_back * older[rows, :] + (weight_here - 1.0) * old[rows, :]
                states[1, rows, :] = states[0, rows, :] + step_size * (
                    rates[0, rows, :] + upper * extra
                )

            sweep(work)

        @on(True, 1)
        def _():
            def work(rows):
                states[2, rows, :] = states[1, rows, :] + step_size * rates[1, rows, :]

            sweep(work)

        @on(True, 2)
        def _():
            def work(rows):
                moved = states[2, rows, :] + step_size * rates[2, rows, :] - states[0, rows, :]
                out[rows, :] = moved * SCALE

            sweep(work)

        @on(False, 2)
        def _():
            def work(rows):
                below = step_size * rates[2, rows, :]
                states[3, rows, :] = states[1, rows, :] + weight_next * below
                states[5, rows, :] = states[2, rows, :] + below

            sweep(work)

        @on(False, 3)
        def _():
            def work(rows):
                states[4, rows, :] = states[3, rows, :] + step_size * (
                    rates[3, rows, :]
                    + weight_back * old[rows, :]
                    + (weight_here - 1.0) * rates[2, rows, :]
                )

            sweep(work)

        @on(False, 5)
        def _():
            def work(rows):
                below = step_size * rates[5, rows, :]
                states[7, rows, :] = states[4, rows, :] + weight_next * below
                states[6, rows, :] = states[5, rows, :] + below

            sweep(work)

        @on(False, 7)
        def _():
            def work(rows):
                change = (
                    rates[7, rows, :]
                    + weight_back * rates[2, rows, :]
                    + (weight_here - 1.0) * rates[5, rows, :]
                    + weight_next * rates[6, rows, :]
                )
                moved = states[7, rows, :] + step_size * change - states[0, rows, :]
                out[rows, :] = moved * SCALE

            sweep(work)

        return carry

    lax.fori_loop(0, STEPS, step, 0)

    @pl.when(base_level)
    def _():
        for stage in range(TSTEPS):
            forwarded(stage).wait_send()


def window_of(fields, indices):
    tiles = lax.axis_size("tile")
    width = fields[0].shape[1]
    faces = indices[3].shape[1]
    full = (SIZE, width)
    f32, bf16 = jnp.float32, jnp.bfloat16
    operands = [*fields, *indices, jnp.asarray(block_numbers())]
    operands = [pltpu.with_memory_space_constraint(x, pltpu.HBM) for x in operands]
    return pl.pallas_call(
        window_kernel,
        out_shape=jax.ShapeDtypeStruct(full, f32),
        in_specs=[pl.BlockSpec(memory_space=pl.ANY)] * len(operands),
        out_specs=VMEM,
        scratch_shapes=[
            pltpu.VMEM((STEPS,) + full, f32),
            pltpu.VMEM((STEPS,) + full, f32),
            pltpu.VMEM(full, f32),
            pltpu.VMEM(full, f32),
            *[pltpu.VMEM(x.shape, x.dtype) for x in operands[5:]],
            pltpu.VMEM((faces, faces), bf16),
            pltpu.VMEM((tiles * FCAP, faces), bf16),
            pltpu.VMEM((tiles * FCAP, faces), bf16),
            pltpu.VMEM((2 * ROWS, faces), bf16),
            pltpu.VMEM(full, f32),
            pltpu.VMEM(full, bf16),
            pltpu.VMEM(full, bf16),
            pltpu.VMEM((6 * ROWS, width), f32),
            pltpu.VMEM((TSTEPS, tiles, FCAP, ROWS), f32),
            pltpu.VMEM((2 * TSTEPS, tiles, FCAP, ROWS), f32),
            pltpu.SemaphoreType.DMA((TSTEPS, tiles)),
            pltpu.SemaphoreType.DMA((TSTEPS, tiles)),
            pltpu.SemaphoreType.DMA((5,)),
            pltpu.SemaphoreType.DMA((6,)),
            pltpu.SemaphoreType.DMA((6,)),
            pltpu.SemaphoreType.DMA((6,)),
        ],
        compiler_params=pltpu.CompilerParams(
            collective_id=2, has_side_effects=True, vmem_limit_bytes=44 << 20
        ),
    )(*operands)


def turning():
    nodes = np.arange(NODES)
    blocks = []
    for orient in range(4):
        source = nodes.reshape(NP, NP)
        if orient >= 2:
            source = source[::-1, ::-1]
        if orient % 2 == 1:
            source = source.T
        block = np.zeros((NODES, NODES), np.float32)
        block[nodes, source.reshape(-1)] = 1.0
        blocks.append(block)
    return np.concatenate(blocks, axis=1)


def body(
    density,
    momentum,
    energy,
    rhs_older,
    rhs_old,
    peer_tile,
    peer_index,
    boundary_slot,
    face_partner,
    face_orient,
):
    width = density.shape[-1]
    if lax.axis_size("level") == 2:
        fields = [density, momentum, energy, rhs_older, rhs_old]
        indices = [peer_tile, peer_index, boundary_slot, face_partner, face_orient]
        result = window_of([field.reshape(-1, width) for field in fields], indices)
        return result.reshape(rhs_old.shape)
    start = jnp.concatenate(
        [
            density.reshape(-1, width),
            momentum.reshape(-1, width),
            energy.reshape(-1, width),
        ],
        axis=0,
    )
    level = lax.axis_index("level")
    tiles = lax.axis_size("tile")
    peers = peer_tile[0]
    matches = peer_index[0]
    slots = boundary_slot[0]
    partner = face_partner[0]
    orient = face_orient[0]
    count = peers.shape[0]
    faces = partner.shape[0]
    same_peer = peers[:, None] == peers[None, :]
    listing = jnp.arange(count, dtype=jnp.int32)
    send_rank = jnp.sum(same_peer & (matches[None, :] < matches[:, None]), axis=1, dtype=jnp.int32)
    recv_rank = jnp.sum(same_peer & (listing[None, :] < listing[:, None]), axis=1, dtype=jnp.int32)
    places = jnp.arange(tiles * FCAP, dtype=jnp.int32)
    ids = jnp.arange(faces, dtype=jnp.int32)
    exact = jnp.bfloat16
    at_slot = (slots[:, None] == ids[None, :]).astype(exact)

    def routing(rank):
        onehot = (places[:, None] == (peers * FCAP + rank)[None, :]).astype(exact)
        return jnp.dot(onehot, at_slot, preferred_element_type=jnp.float32).astype(exact)

    send = routing(send_rank)
    place = routing(recv_rank)
    inner = ((ids[:, None] == partner[None, :]) & (partner != ids)[None, :]).astype(exact)
    masks = (orient[None, :] == jnp.arange(8, dtype=jnp.int32)[:, None]).astype(jnp.float32)
    turn = jnp.asarray(turning(), exact)
    numbers = derivative_numbers()
    diagonals = np.stack(
        [
            np.stack([-metric * numbers[k, (k + shift) % NP] for k in range(NP)])
            for shift in range(NP)
        ]
    ).astype(np.float32)
    rolled = jnp.broadcast_to(jnp.asarray(diagonals)[:, :, None], (NP, NP, width))

    tables = (masks, turn, inner, send, place, rolled)

    def rates(states):
        return rates_of(states, tables)

    older = rhs_older.reshape(-1, width)
    old = rhs_old.reshape(-1, width)

    def advance(state, own_rate, older, old, below):
        corrected = (
            state
            + step_size * (own_rate - old)
            + step_size * (weight_back * older + weight_here * old + weight_next * below)
        )
        return jnp.where(level == 0, state + step_size * own_rate, corrected)

    state = start
    for repeat in range(TSTEPS):
        own_rate = rates([state])[0]
        below = shifted(own_rate, "level", 1)
        state = advance(state, own_rate, older, old, below)
        older = old
        old = below
    return ((state - start) / (TSTEPS * step_size)).reshape(rhs_old.shape)


def solution(mesh):
    return jax.shard_map(
        body,
        mesh=mesh,
        in_specs=(
            P("level", None, None, None, "tile"),
            P("level", None, None, None, None, "tile"),
            P("level", None, None, None, "tile"),
            P("level", None, None, None, None, "tile"),
            P("level", None, None, None, None, "tile"),
            P("tile", None),
            P("tile", None),
            P("tile", None),
            P("tile", None),
            P("tile", None),
        ),
        out_specs=P("level", None, None, None, None, "tile"),
        check_vma=False,
    )
```

```python
import functools

import jax
import jax.numpy as jnp
import numpy as np
from jax import lax
from jax.experimental import pallas as pl
from jax.experimental.pallas import tpu as pltpu
from jax.sharding import PartitionSpec as P

NP = 8
TSTEPS = 3
FCAP = 8


step_size = 0.02
penalty = 2.5
metric = 0.1
lift_factor = 2.8
weight_back = -1.0 / 12.0
weight_here = 8.0 / 12.0
weight_next = 5.0 / 12.0


def shifted(block, axis, distance):
    devices = range(lax.axis_size(axis))
    route = [(i - distance, i) for i in devices if i - distance in devices]
    return lax.ppermute(block, axis, route)


def lobatto_points():
    degree = NP - 1
    points = np.cos(np.pi * np.arange(degree + 1) / degree)
    table = np.zeros((degree + 1, degree + 1))
    for sweep in range(60):
        table[:, 0] = 1.0
        table[:, 1] = points
        for order in range(2, degree + 1):
            table[:, order] = (
                (2 * order - 1) * points * table[:, order - 1] - (order - 1) * table[:, order - 2]
            ) / order
        points = points - (points * table[:, degree] - table[:, degree - 1]) / (
            (degree + 1) * table[:, degree]
        )
    table[:, 0] = 1.0
    table[:, 1] = points
    for order in range(2, degree + 1):
        table[:, order] = (
            (2 * order - 1) * points * table[:, order - 1] - (order - 1) * table[:, order - 2]
        ) / order
    return (points[::-1], table[::-1, degree])


def derivative_numbers():
    degree = NP - 1
    points, values = lobatto_points()
    identity = np.eye(NP)
    spread = points[:, None] - points[None, :] + identity
    table = values[:, None] / values[None, :] / spread
    table = table * (1.0 - identity)
    table[0, 0] = -degree * (degree + 1) / 4.0
    table[degree, degree] = degree * (degree + 1) / 4.0
    return np.asarray(table, dtype=np.float32)

NV = 5
NODES = NP * NP
ROWS = NV * NODES
SIZE = NV * NP * NODES
CELLS = NP * NODES
STEPS = 8
SCALE = 1.0 / (TSTEPS * step_size)


def primitive(w):
    inverse = 1.0 / w[0]
    velocity = [w[c] * inverse for c in (1, 2, 3)]
    pressure = 0.4 * (w[4] - 0.5 * (w[1] * velocity[0] + w[2] * velocity[1] + w[3] * velocity[2]))
    return velocity, pressure


def flux(w, velocity, pressure, direction):
    carried = w[1 + direction]
    parts = [carried]
    for column in range(3):
        product = carried * velocity[column]
        if column == direction:
            product = product + pressure
        parts.append(product)
    parts.append((w[4] + pressure) * velocity[direction])
    return parts


def pieces_of(x):
    high = x.astype(jnp.bfloat16)
    rest = x - high.astype(jnp.float32)
    middle = rest.astype(jnp.bfloat16)
    low = (rest - middle.astype(jnp.float32)).astype(jnp.bfloat16)
    return [high, middle, low]


def face_rows(which):
    direction, end = which // 2, (NP - 1) * (which % 2)
    return direction, end


def trace_rows(ref, which, v):
    direction, end = face_rows(which)
    base = v * NP * NODES
    if direction == 0:
        return ref[pl.ds(base + end * NODES, NODES), :]
    if direction == 1:
        return jnp.concatenate(
            [ref[pl.ds(base + i * NODES + end * NP, NP), :] for i in range(NP)], axis=0
        )
    return ref[pl.ds(base + end, NODES, stride=NP), :]


def gather_traces(state, masks, turn, turned):
    width = state.shape[1]
    for which in range(6):
        lanes = pl.ds(which * width, width)
        mask = [jnp.broadcast_to(masks[o : o + 1, lanes], (NODES, width)) for o in range(4)]
        for v in range(NV):
            for at, piece in enumerate(pieces_of(trace_rows(state, which, v))):
                wide = piece.astype(jnp.float32)
                stacked = jnp.concatenate([(wide * m).astype(jnp.bfloat16) for m in mask], axis=0)
                out = jnp.dot(turn[...], stacked, preferred_element_type=jnp.float32)
                turned[at, pl.ds(v * NODES, NODES), lanes] = out.astype(jnp.bfloat16)


def outgoing_of(turned, send):
    outgoing = None
    for at in range(3):
        leave = lax.dot_general(
            send[...], turned[at], (((1,), (1,)), ((), ())), preferred_element_type=jnp.float32
        )
        outgoing = leave if outgoing is None else outgoing + leave
    return outgoing


def inner_of(turned, inner):
    total = None
    for at in range(3):
        part = jnp.dot(turned[at], inner[...], preferred_element_type=jnp.float32)
        total = part if total is None else total + part
    return total


def outer_of(arrived, place):
    total = None
    for piece in pieces_of(arrived):
        part = lax.dot_general(
            piece, place[...], (((0,), (0,)), ((), ())), preferred_element_type=jnp.float32
        )
        total = part if total is None else total + part
    return total


def volume_of(state, rolled, rate):
    numbers = derivative_numbers()

    def derived(fields):
        even = [fields[index] + fields[NP - 1 - index] for index in range(NP // 2)]
        odd = [fields[index] - fields[NP - 1 - index] for index in range(NP // 2)]
        results = [None] * NP
        for target in range(NP // 2):
            near = None
            far = None
            for index in range(NP // 2):
                here = float(numbers[target, index])
                there = float(numbers[target, NP - 1 - index])
                one = (-0.5 * metric * (here + there)) * even[index]
                two = (-0.5 * metric * (here - there)) * odd[index]
                near = one if near is None else near + one
                far = two if far is None else far + two
            results[target] = far + near
            results[NP - 1 - target] = far - near
        return results

    def at(v, i, j):
        return pl.ds(pl.multiple_of(v * NP * NODES + i * NODES + j * NP, NP), NP)

    def along_first(j, carry):
        across = [[None] * NP for v in range(NV)]
        down = [[None] * NP for v in range(NV)]
        for i in range(NP):
            w = [state[at(v, i, j), :] for v in range(NV)]
            velocity, pressure = primitive(w)
            for v, part in enumerate(flux(w, velocity, pressure, 0)):
                across[v][i] = part
            for v, part in enumerate(flux(w, velocity, pressure, 2)):
                total = rolled[0] * part
                for shift in range(1, NP):
                    total = total + rolled[shift] * pltpu.roll(part, NP - shift, 0)
                down[v][i] = total
        for v in range(NV):
            for i, part in enumerate(derived(across[v])):
                rate[at(v, i, j), :] = part + down[v][i]
        return carry

    def along_second(i, carry):
        across = [[None] * NP for v in range(NV)]
        for j in range(NP):
            w = [state[at(v, i, j), :] for v in range(NV)]
            velocity, pressure = primitive(w)
            for v, part in enumerate(flux(w, velocity, pressure, 1)):
                across[v][j] = part
        for v in range(NV):
            for j, part in enumerate(derived(across[v])):
                rate[at(v, i, j), :] = rate[at(v, i, j), :] + part
        return carry

    lax.fori_loop(0, NP, along_first, 0)
    lax.fori_loop(0, NP, along_second, 0)


def lift_faces(state, view, rate):
    width = state.shape[1]
    for which in range(6):
        direction, end = face_rows(which)
        normal = 2.0 * (which % 2) - 1.0
        lanes = pl.ds(which * width, width)

        def lift(row, carry):
            def rows(v):
                base = v * NP * NODES
                if direction == 0:
                    return pl.ds(pl.multiple_of(base + end * NODES + row * NP, NP), NP)
                if direction == 1:
                    return pl.ds(pl.multiple_of(base + row * NODES + end * NP, NP), NP)
                return pl.ds(base + row * NODES + end, NP, stride=NP)

            own = [state[rows(v), :] for v in range(NV)]
            far = [
                view[pl.ds(pl.multiple_of(v * NODES + row * NP, NP), NP), lanes]
                for v in range(NV)
            ]
            own_flux = flux(own, *primitive(own), direction)
            far_flux = flux(far, *primitive(far), direction)
            for v in range(NV):
                jump = (0.5 * normal) * (far_flux[v] - own_flux[v]) - (0.5 * penalty) * (
                    far[v] - own[v]
                )
                rate[rows(v), :] = rate[rows(v), :] - lift_factor * jump
            return carry

        lax.fori_loop(0, NP, lift, 0)


VMEM = pl.BlockSpec(memory_space=pltpu.VMEM)


def rate_kernel(count, *refs):
    states, refs = refs[:count], refs[count:]
    masks, turn, inner, send, place, rolled = refs[:6]
    rates, refs = refs[6 : 6 + count], refs[6 + count :]
    turned, views, buffer, landed, send_sem, recv_sem = refs
    tiles = lax.axis_size("tile")
    me = lax.axis_index("tile")
    barrier = pltpu.get_barrier_semaphore()

    def peer(offset):
        return {"tile": lax.rem(me + offset, tiles)}

    def copy(offset):
        return pltpu.make_async_remote_copy(
            src_ref=buffer.at[lax.rem(me + offset, tiles)],
            dst_ref=landed.at[me],
            send_sem=send_sem.at[offset],
            recv_sem=recv_sem.at[offset],
            device_id=peer(offset),
            device_id_type=pl.DeviceIdType.MESH,
        )

    def greet(offset, carry):
        pl.semaphore_signal(
            barrier, inc=1, device_id=peer(offset), device_id_type=pl.DeviceIdType.MESH
        )
        return carry

    def begin(offset, carry):
        copy(offset).start()
        return carry

    def finish(offset, carry):
        copy(offset).wait()
        return carry

    lax.fori_loop(1, tiles, greet, 0)
    for at in range(count):
        gather_traces(states[at], masks, turn, turned.at[at])
        leave = outgoing_of(turned.at[at], send)
        buffer[:, at * FCAP : (at + 1) * FCAP, :] = leave.reshape(tiles, FCAP, ROWS)
    pl.semaphore_wait(barrier, tiles - 1)
    lax.fori_loop(1, tiles, begin, 0)
    landed[me] = jnp.zeros(landed.shape[1:], jnp.float32)
    for at in range(count):
        views[at] = inner_of(turned.at[at], inner)
        volume_of(states[at], rolled, rates[at])
    lax.fori_loop(1, tiles, finish, 0)
    for at in range(count):
        arrived = landed[:, at * FCAP : (at + 1) * FCAP, :].reshape(tiles * FCAP, ROWS)
        views[at] = views[at] + outer_of(arrived, place)
        lift_faces(states[at], views.at[at], rates[at])


def rates_of(states, tables):
    tiles = lax.axis_size("tile")
    count = len(states)
    slots = tables[0].shape[1]
    like = jax.ShapeDtypeStruct(states[0].shape, jnp.float32)
    return pl.pallas_call(
        functools.partial(rate_kernel, count),
        out_shape=[like] * count,
        in_specs=[VMEM] * (count + len(tables)),
        out_specs=[VMEM] * count,
        scratch_shapes=[
            pltpu.VMEM((count, 3, ROWS, slots), jnp.bfloat16),
            pltpu.VMEM((count, ROWS, slots), jnp.float32),
            pltpu.VMEM((tiles, count * FCAP, ROWS), jnp.float32),
            pltpu.VMEM((tiles, count * FCAP, ROWS), jnp.float32),
            pltpu.SemaphoreType.DMA((tiles,)),
            pltpu.SemaphoreType.DMA((tiles,)),
        ],
        compiler_params=pltpu.CompilerParams(
            collective_id=count - 1, has_side_effects=True, vmem_limit_bytes=40 << 20
        ),
    )(*states, *tables)


def pieces_pair(x):
    high = x.astype(jnp.bfloat16)
    return high, (x - high.astype(jnp.float32)).astype(jnp.bfloat16)


def fluxes(w):
    inverse = 1.0 / w[0]
    velocity = [w[c] * inverse for c in (1, 2, 3)]
    product = {}
    for a in range(3):
        for b in range(a, 3):
            product[a, b] = product[b, a] = w[1 + a] * velocity[b]
    pressure = 0.4 * (w[4] - 0.5 * (product[0, 0] + product[1, 1] + product[2, 2]))
    total = w[4] + pressure
    return [
        [w[1 + d]]
        + [product[d, c] + pressure if c == d else product[d, c] for c in range(3)]
        + [total * velocity[d]]
        for d in range(3)
    ]


def derived(fields):
    numbers = derivative_numbers()
    even = [fields[index] + fields[NP - 1 - index] for index in range(NP // 2)]
    odd = [fields[index] - fields[NP - 1 - index] for index in range(NP // 2)]
    results = [None] * NP
    for target in range(NP // 2):
        near = None
        far = None
        for index in range(NP // 2):
            here = float(numbers[target, index])
            there = float(numbers[target, NP - 1 - index])
            one = (-0.5 * metric * (here + there)) * even[index]
            two = (-0.5 * metric * (here - there)) * odd[index]
            near = one if near is None else near + one
            far = two if far is None else far + two
        results[target] = far + near
        results[NP - 1 - target] = far - near
    return results


GROUP = 2 * NODES


def block_numbers():
    whole = np.kron(np.eye(GROUP // NP), -metric * derivative_numbers()).astype(np.float32)
    high = whole.astype(jnp.bfloat16)
    low = (whole - high.astype(np.float32)).astype(jnp.bfloat16)
    return np.concatenate([high, low, high], axis=1)


def spread_traces(state, spread, variables=range(NV)):
    width = state.shape[1]
    for which in range(6):
        lanes = pl.ds(which * width, width)
        for v in variables:
            high, low = pieces_pair(trace_rows(state, which, v))
            spread[pl.ds(v * NODES, NODES), lanes] = high
            spread[pl.ds(ROWS + v * NODES, NODES), lanes] = low


def node_rows(v, i, j, count=NP):
    return pl.ds(v * NP * NODES + i * NODES + j * NP, count)


def planes_and_views(state, spread, inner, flow, high, low, rate, view):
    width = state.shape[1]
    for i in range(NP):
        across = [[None] * NP for v in range(NV)]
        for j in range(0, NP, 2):
            thirds = [None, None]
            for half in range(2):
                w = [state[node_rows(v, i, j + half), :] for v in range(NV)]
                one, two, thirds[half] = fluxes(w)
                for v in range(NV):
                    across[v][j + half] = two[v]
                    flow[node_rows(v, i, j + half), :] = one[v]
            for v in range(NV):
                both = jnp.concatenate([thirds[0][v], thirds[1][v]], axis=0)
                upper, lower = pieces_pair(both)
                high[node_rows(v, i, j, 2 * NP), :] = upper
                low[node_rows(v, i, j, 2 * NP), :] = lower
        for v in range(NV):
            for j, part in enumerate(derived(across[v])):
                rate[node_rows(v, i, j), :] = part
        if i % 2 == 0 and i < 6:
            both = jnp.dot(
                spread[...], inner[:, i * width : (i + 2) * width],
                preferred_element_type=jnp.float32,
            )
            both = both[:ROWS] + both[ROWS:]
            for half in range(2):
                view[pl.ds((i + half) * ROWS, ROWS), :] = both[:, half * width : (half + 1) * width]


def remaining_volume(flow, high, low, blocks, rate):
    width = flow.shape[1]
    many = GROUP // NODES
    for v in range(NV):
        down = [None] * NP
        for i in range(0, NP // 2, many):

            def pair(ref):
                sides = [ref[node_rows(v, at, 0, GROUP), :] for at in (i, i + NP // 2)]
                return jnp.concatenate(sides, axis=1)

            upper, lower = pair(high), pair(low)
            both = jnp.dot(
                blocks[...],
                jnp.concatenate([upper, upper, lower], axis=0),
                preferred_element_type=jnp.float32,
            )
            for at in range(many):
                part = both[at * NODES : (at + 1) * NODES, :]
                down[i + at], down[i + at + NP // 2] = part[:, :width], part[:, width:]
        for j in range(NP):
            parts = derived([flow[node_rows(v, i, j), :] for i in range(NP)])
            for i, part in enumerate(parts):
                rows = node_rows(v, i, j)
                rate[rows, :] = rate[rows, :] + part + down[i][j * NP : (j + 1) * NP, :]


def lift_all(state, view, traces, place, orient, rate):
    width = state.shape[1]
    upper, lower = pieces_pair(traces.T)
    sides = jnp.concatenate([upper, lower], axis=0)
    ahead = lax.broadcasted_iota(jnp.int32, (NP, width), 0)
    for which in range(6):
        direction, end = face_rows(which)
        normal = 2.0 * (which % 2) - 1.0
        lanes = pl.ds(which * width, width)
        if which % 2 == 0:
            outer = jnp.dot(
                sides, place[:, which * width : (which + 2) * width],
                preferred_element_type=jnp.float32,
            )
            outer = outer[:ROWS] + outer[ROWS:]
            for half in range(2):
                rows = pl.ds((which + half) * ROWS, ROWS)
                view[rows, :] = view[rows, :] + outer[:, half * width : (half + 1) * width]
        orients = jnp.broadcast_to(orient[0:1, lanes], (NP, width))
        crossed = (orients & 1) == 1
        turned = orients >= 2
        order = jnp.where(turned, NP - 1 - ahead, ahead)

        def rows_of(v, row):
            base = v * NP * NODES
            if direction == 0:
                return pl.ds(base + end * NODES + row * NP, NP)
            if direction == 1:
                return pl.ds(base + row * NODES + end * NP, NP)
            return pl.ds(base + row * NODES + end, NP, stride=NP)

        for near in range(NP // 2):
            pair = [near, NP - 1 - near]
            far = [[], []]
            for v in range(NV):
                base = which * ROWS + v * NODES
                seen = [
                    jnp.where(
                        crossed,
                        view[pl.ds(base + row, NP, stride=NP), :],
                        view[pl.ds(base + row * NP, NP), :],
                    )
                    for row in pair
                ]
                for half in range(2):
                    picked = jnp.where(turned, seen[1 - half], seen[half])
                    far[half].append(
                        jnp.take_along_axis(picked, order, axis=0, mode="promise_in_bounds")
                    )
            for half in range(2):
                rows = [rows_of(v, pair[half]) for v in range(NV)]
                own = [state[rows[v], :] for v in range(NV)]
                own_flux = flux(own, *primitive(own), direction)
                far_flux = flux(far[half], *primitive(far[half]), direction)
                for v in range(NV):
                    jump = (0.5 * normal) * (far_flux[v] - own_flux[v]) - (0.5 * penalty) * (
                        far[half][v] - own[v]
                    )
                    rate[rows[v], :] = rate[rows[v], :] - lift_factor * jump


def table_rows(ref, fill):
    row = ref[...].astype(jnp.float32)
    extra = -row.shape[1] % 128
    if extra > 0:
        row = jnp.concatenate([row, jnp.full((1, extra), fill, jnp.float32)], axis=1)
    return row


def fill_tables(peers, matches, slots, partner, inner, send, place):
    faces = partner.shape[1]
    pack = 16

    def some(at, carry):
        base = pl.multiple_of(at * pack, pack)
        ids = lax.broadcasted_iota(jnp.int32, (pack, faces), 0) + base
        lane = lax.broadcasted_iota(jnp.int32, (pack, faces), 1)
        mate = jnp.broadcast_to(partner[...], (pack, faces))
        hit = jnp.where((ids == mate) & (mate != lane), 1.0, 0.0)
        inner[pl.ds(base, pack), :] = hit.astype(jnp.bfloat16)
        return carry

    lax.fori_loop(0, faces // pack, some, 0)
    peer = table_rows(peers, -1.0)
    match = table_rows(matches, -1.0)
    slot = table_rows(slots, -1.0)
    count = peer.shape[1]
    square = (count, count)
    peer_across = jnp.broadcast_to(peer, square)
    match_across = jnp.broadcast_to(match, square)
    same = peer_across.T == peer_across
    lower = match_across.T < match_across
    sooner = lax.broadcasted_iota(jnp.int32, square, 0) < lax.broadcasted_iota(jnp.int32, square, 1)
    slot_of = lax.broadcasted_iota(jnp.int32, (faces, count), 0).astype(jnp.float32)
    at_slot = jnp.where(slot_of == jnp.broadcast_to(slot, (faces, count)), 1.0, 0.0)
    at_slot = at_slot.astype(jnp.bfloat16)
    places = send.shape[0]
    spots = lax.broadcasted_iota(jnp.int32, (places, count), 0).astype(jnp.float32)
    for ahead, table in ((lower, send), (sooner, place)):
        rank = jnp.sum(jnp.where(same & ahead, 1.0, 0.0), axis=0, keepdims=True)
        spot = jnp.broadcast_to(peer * FCAP + rank, (places, count))
        onehot = jnp.where(spots == spot, 1.0, 0.0).astype(jnp.bfloat16)
        routed = lax.dot_general(
            onehot, at_slot, (((1,), (1,)), ((), ())), preferred_element_type=jnp.float32
        )
        table[...] = routed.astype(jnp.bfloat16)


def window_kernel(*refs):
    fields, refs = refs[:5], refs[5:]
    indices, refs = refs[:6], refs[6:]
    out, refs = refs[0], refs[1:]
    states, rates, older, old, refs = refs[0], refs[1], refs[2], refs[3], refs[4:]
    held, refs = refs[:6], refs[6:]
    inner, send, place, spread, flow, high, low, view, refs = *refs[:8], refs[8:]
    parcels, landings, refs = refs[:2], refs[2:4], refs[4:]
    buffer, traces, send_sem, recv_sem, load_sem, table_sem, pass_send, pass_recv = refs
    peers, matches, slots, partner, orient, blocks = held
    tiles = lax.axis_size("tile")
    me = lax.axis_index("tile")
    level = lax.axis_index("level")
    base_level = level == 0
    upper = (level > 0).astype(jnp.float32)
    other = {"level": 1 - level}
    barrier = pltpu.get_barrier_semaphore()
    parts = [
        (fields[0], 0, CELLS),
        (fields[1], CELLS, 3 * CELLS),
        (fields[2], 4 * CELLS, CELLS),
    ]

    def peer(offset):
        return {"tile": lax.rem(me + offset, tiles)}

    def swap(stage, offset):
        return pltpu.make_async_remote_copy(
            src_ref=buffer.at[stage, lax.rem(me + offset, tiles)],
            dst_ref=traces.at[stage, me],
            send_sem=send_sem.at[stage, offset],
            recv_sem=recv_sem.at[stage, offset],
            device_id=peer(offset),
            device_id_type=pl.DeviceIdType.MESH,
        )

    def portion(at, offset):
        return pltpu.make_async_remote_copy(
            src_ref=parcels[at].at[lax.rem(me + offset, tiles)],
            dst_ref=landings[at].at[me],
            send_sem=send_sem.at[TSTEPS + at, offset],
            recv_sem=recv_sem.at[TSTEPS + at, offset],
            device_id=peer(offset),
            device_id_type=pl.DeviceIdType.MESH,
        )

    def handed(at):
        ref, base, count = parts[at]
        return pltpu.make_async_remote_copy(
            src_ref=ref,
            dst_ref=states.at[2, pl.ds(base, count), :],
            send_sem=pass_send.at[at],
            recv_sem=pass_recv.at[at],
            device_id=other,
            device_id_type=pl.DeviceIdType.MESH,
        )

    def forwarded(stage):
        return pltpu.make_async_remote_copy(
            src_ref=traces.at[stage],
            dst_ref=traces.at[TSTEPS + stage],
            send_sem=pass_send.at[3 + stage],
            recv_sem=pass_recv.at[3 + stage],
            device_id=other,
            device_id_type=pl.DeviceIdType.MESH,
        )

    def greet(offset, carry):
        pl.semaphore_signal(
            barrier, inc=1, device_id=peer(offset), device_id_type=pl.DeviceIdType.MESH
        )
        return carry

    pl.semaphore_signal(barrier, inc=1, device_id=other, device_id_type=pl.DeviceIdType.MESH)
    lax.fori_loop(1, tiles, greet, 0)
    tables = [
        pltpu.make_async_copy(ref, kept, table_sem.at[at])
        for at, (ref, kept) in enumerate(zip(indices, held))
    ]
    loads = [
        pltpu.make_async_copy(ref, states.at[0, pl.ds(base, count), :], load_sem.at[at])
        for at, (ref, base, count) in enumerate(parts)
    ]
    loads.append(pltpu.make_async_copy(fields[3], older, load_sem.at[3]))
    loads.append(pltpu.make_async_copy(fields[4], old, load_sem.at[4]))
    for load in tables + loads:
        load.start()
    pl.semaphore_wait(barrier, tiles)

    @pl.when(base_level)
    def _():
        for at in range(3):
            handed(at).start()

    for load in tables:
        load.wait()
    fill_tables(peers, matches, slots, partner, inner, send, place)
    for stage in range(TSTEPS):
        traces[stage, me] = jnp.zeros(traces.shape[2:], jnp.float32)
    for landing in landings:
        landing[me] = jnp.zeros(landing.shape[1:], jnp.float32)
    for load in loads:
        load.wait()

    def arrive(stage):
        def finish(offset, carry):
            swap(stage, offset).wait()
            return carry

        lax.fori_loop(1, tiles, finish, 0)

    def sweep(work):
        rows = SIZE // 20

        def chunk(at, carry):
            work(pl.ds(pl.multiple_of(at * rows, rows), rows))
            return carry

        lax.fori_loop(0, 20, chunk, 0)

    def share_out(at, state, variables):
        spread_traces(state, spread, variables)
        leave = None
        for half in range(2):
            rows = pl.ds(half * ROWS + variables[0] * NODES, len(variables) * NODES)
            part = lax.dot_general(
                send[...], spread[rows, :], (((1,), (1,)), ((), ())),
                preferred_element_type=jnp.float32,
            )
            leave = part if leave is None else leave + part
        parcels[at][...] = leave.reshape(parcels[at].shape)

        def begin(offset, carry):
            portion(at, offset).start()
            return carry

        lax.fori_loop(1, tiles, begin, 0)

    def collect(at):
        def finish(offset, carry):
            portion(at, offset).wait()
            return carry

        lax.fori_loop(1, tiles, finish, 0)

    def step(t, carry):
        def on(base, at):
            return pl.when((level == 0) & (t == at) if base else (level > 0) & (t == at))

        state, rate = states.at[t], rates.at[t]
        stage = jnp.where(t <= 1, t, 2)
        leaving = jnp.where(base_level, t <= 2, (t <= 1) | (t == 4))
        lasting = jnp.where(base_level, t <= 2, (t != 1) & (t != 4))

        @on(False, 2)
        def _():
            for at in range(2):
                handed(at).wait_recv()
            share_out(0, state, range(NV - 1))
            handed(2).wait_recv()
            share_out(1, state, range(NV - 1, NV))

        @pl.when((leaving | lasting) & (base_level | (t != 2)))
        def _():
            spread_traces(state, spread)

        @pl.when(leaving)
        def _():
            leave = lax.dot_general(
                send[...], spread[...], (((1,), (1,)), ((), ())), preferred_element_type=jnp.float32
            )
            leave = leave[:, :ROWS] + leave[:, ROWS:]
            buffer[stage] = leave.reshape(tiles, FCAP, ROWS)

            def begin(offset, carry):
                swap(stage, offset).start()
                return carry

            lax.fori_loop(1, tiles, begin, 0)

        @pl.when(lasting)
        def _():
            planes_and_views(state, spread, inner, flow, high, low, rate, view)
            remaining_volume(flow, high, low, blocks, rate)

            @pl.when(base_level | (t == 0))
            def _():
                arrive(stage)

            @on(True, 2)
            def _():
                for at in range(3):
                    handed(at).wait_send()
                forwarded(1).start()
                forwarded(2).start()

            @on(False, 2)
            def _():
                for at in range(2):
                    collect(at)
                traces[TSTEPS] = jnp.concatenate(
                    [landing[...] for landing in landings], axis=2
                )

            @on(False, 3)
            def _():
                arrive(1)
                forwarded(1).wait_recv()

            @on(False, 6)
            def _():
                forwarded(2).wait_recv()

            @on(False, 7)
            def _():
                arrive(2)

            own = jnp.where(
                base_level | (t == 0),
                t,
                jnp.where(t == 3, 1, jnp.where(t == 7, 2, jnp.where(t == 2, 3, t - 1))),
            )
            mixed = (level > 0) & ((t == 3) | (t == 7))
            newer = jnp.where(mixed, jnp.where(t == 3, 4, 5), own)
            elder = jnp.where(mixed, newer - 1, own)
            share = jnp.where(mixed, weight_next, 0.0)
            seen = traces[own] + share * (traces[newer] - traces[elder])
            lift_all(state, view, seen.reshape(tiles * FCAP, ROWS), place, orient, rate)

        @pl.when(t == 0)
        def _():
            def work(rows):
                extra = weight_back * older[rows, :] + (weight_here - 1.0) * old[rows, :]
                states[1, rows, :] = states[0, rows, :] + step_size * (
                    rates[0, rows, :] + upper * extra
                )

            sweep(work)

        @on(True, 1)
        def _():
            def work(rows):
                states[2, rows, :] = states[1, rows, :] + step_size * rates[1, rows, :]

            sweep(work)

        @on(True, 2)
        def _():
            def work(rows):
                moved = states[2, rows, :] + step_size * rates[2, rows, :] - states[0, rows, :]
                out[rows, :] = moved * SCALE

            sweep(work)

        @on(False, 2)
        def _():
            def work(rows):
                below = step_size * rates[2, rows, :]
                states[3, rows, :] = states[1, rows, :] + weight_next * below
                states[5, rows, :] = states[2, rows, :] + below

            sweep(work)

        @on(False, 3)
        def _():
            def work(rows):
                states[4, rows, :] = states[3, rows, :] + step_size * (
                    rates[3, rows, :]
                    + weight_back * old[rows, :]
                    + (weight_here - 1.0) * rates[2, rows, :]
                )

            sweep(work)

        @on(False, 5)
        def _():
            def work(rows):
                below = step_size * rates[5, rows, :]
                states[7, rows, :] = states[4, rows, :] + weight_next * below
                states[6, rows, :] = states[5, rows, :] + below

            sweep(work)

        @on(False, 7)
        def _():
            def work(rows):
                change = (
                    rates[7, rows, :]
                    + weight_back * rates[2, rows, :]
                    + (weight_here - 1.0) * rates[5, rows, :]
                    + weight_next * rates[6, rows, :]
                )
                moved = states[7, rows, :] + step_size * change - states[0, rows, :]
                out[rows, :] = moved * SCALE

            sweep(work)

        return carry

    lax.fori_loop(0, STEPS, step, 0)

    @pl.when(base_level)
    def _():
        for stage in range(1, TSTEPS):
            forwarded(stage).wait_send()


def window_of(fields, indices):
    tiles = lax.axis_size("tile")
    width = fields[0].shape[1]
    faces = indices[3].shape[1]
    full = (SIZE, width)
    f32, bf16 = jnp.float32, jnp.bfloat16
    operands = [*fields, *indices, jnp.asarray(block_numbers())]
    operands = [pltpu.with_memory_space_constraint(x, pltpu.HBM) for x in operands]
    return pl.pallas_call(
        window_kernel,
        out_shape=jax.ShapeDtypeStruct(full, f32),
        in_specs=[pl.BlockSpec(memory_space=pl.ANY)] * len(operands),
        out_specs=VMEM,
        scratch_shapes=[
            pltpu.VMEM((STEPS,) + full, f32),
            pltpu.VMEM((STEPS,) + full, f32),
            pltpu.VMEM(full, f32),
            pltpu.VMEM(full, f32),
            *[pltpu.VMEM(x.shape, x.dtype) for x in operands[5:]],
            pltpu.VMEM((faces, faces), bf16),
            pltpu.VMEM((tiles * FCAP, faces), bf16),
            pltpu.VMEM((tiles * FCAP, faces), bf16),
            pltpu.VMEM((2 * ROWS, faces), bf16),
            pltpu.VMEM(full, f32),
            pltpu.VMEM(full, bf16),
            pltpu.VMEM(full, bf16),
            pltpu.VMEM((6 * ROWS, width), f32),
            *[pltpu.VMEM((tiles, FCAP, many * NODES), f32) for many in (NV - 1, 1, NV - 1, 1)],
            pltpu.VMEM((TSTEPS, tiles, FCAP, ROWS), f32),
            pltpu.VMEM((2 * TSTEPS, tiles, FCAP, ROWS), f32),
            pltpu.SemaphoreType.DMA((TSTEPS + 2, tiles)),
            pltpu.SemaphoreType.DMA((TSTEPS + 2, tiles)),
            pltpu.SemaphoreType.DMA((5,)),
            pltpu.SemaphoreType.DMA((6,)),
            pltpu.SemaphoreType.DMA((6,)),
            pltpu.SemaphoreType.DMA((6,)),
        ],
        compiler_params=pltpu.CompilerParams(
            collective_id=2, has_side_effects=True, vmem_limit_bytes=44 << 20
        ),
    )(*operands)


def turning():
    nodes = np.arange(NODES)
    blocks = []
    for orient in range(4):
        source = nodes.reshape(NP, NP)
        if orient >= 2:
            source = source[::-1, ::-1]
        if orient % 2 == 1:
            source = source.T
        block = np.zeros((NODES, NODES), np.float32)
        block[nodes, source.reshape(-1)] = 1.0
        blocks.append(block)
    return np.concatenate(blocks, axis=1)


def body(
    density,
    momentum,
    energy,
    rhs_older,
    rhs_old,
    peer_tile,
    peer_index,
    boundary_slot,
    face_partner,
    face_orient,
):
    width = density.shape[-1]
    if lax.axis_size("level") == 2:
        fields = [density, momentum, energy, rhs_older, rhs_old]
        indices = [peer_tile, peer_index, boundary_slot, face_partner, face_orient]
        result = window_of([field.reshape(-1, width) for field in fields], indices)
        return result.reshape(rhs_old.shape)
    start = jnp.concatenate(
        [
            density.reshape(-1, width),
            momentum.reshape(-1, width),
            energy.reshape(-1, width),
        ],
        axis=0,
    )
    level = lax.axis_index("level")
    tiles = lax.axis_size("tile")
    peers = peer_tile[0]
    matches = peer_index[0]
    slots = boundary_slot[0]
    partner = face_partner[0]
    orient = face_orient[0]
    count = peers.shape[0]
    faces = partner.shape[0]
    same_peer = peers[:, None] == peers[None, :]
    listing = jnp.arange(count, dtype=jnp.int32)
    send_rank = jnp.sum(same_peer & (matches[None, :] < matches[:, None]), axis=1, dtype=jnp.int32)
    recv_rank = jnp.sum(same_peer & (listing[None, :] < listing[:, None]), axis=1, dtype=jnp.int32)
    places = jnp.arange(tiles * FCAP, dtype=jnp.int32)
    ids = jnp.arange(faces, dtype=jnp.int32)
    exact = jnp.bfloat16
    at_slot = (slots[:, None] == ids[None, :]).astype(exact)

    def routing(rank):
        onehot = (places[:, None] == (peers * FCAP + rank)[None, :]).astype(exact)
        return jnp.dot(onehot, at_slot, preferred_element_type=jnp.float32).astype(exact)

    send = routing(send_rank)
    place = routing(recv_rank)
    inner = ((ids[:, None] == partner[None, :]) & (partner != ids)[None, :]).astype(exact)
    masks = (orient[None, :] == jnp.arange(8, dtype=jnp.int32)[:, None]).astype(jnp.float32)
    turn = jnp.asarray(turning(), exact)
    numbers = derivative_numbers()
    diagonals = np.stack(
        [
            np.stack([-metric * numbers[k, (k + shift) % NP] for k in range(NP)])
            for shift in range(NP)
        ]
    ).astype(np.float32)
    rolled = jnp.broadcast_to(jnp.asarray(diagonals)[:, :, None], (NP, NP, width))

    tables = (masks, turn, inner, send, place, rolled)

    def rates(states):
        return rates_of(states, tables)

    older = rhs_older.reshape(-1, width)
    old = rhs_old.reshape(-1, width)

    def advance(state, own_rate, older, old, below):
        corrected = (
            state
            + step_size * (own_rate - old)
            + step_size * (weight_back * older + weight_here * old + weight_next * below)
        )
        return jnp.where(level == 0, state + step_size * own_rate, corrected)

    state = start
    for repeat in range(TSTEPS):
        own_rate = rates([state])[0]
        below = shifted(own_rate, "level", 1)
        state = advance(state, own_rate, older, old, below)
        older = old
        old = below
    return ((state - start) / (TSTEPS * step_size)).reshape(rhs_old.shape)


def solution(mesh):
    return jax.shard_map(
        body,
        mesh=mesh,
        in_specs=(
            P("level", None, None, None, "tile"),
            P("level", None, None, None, None, "tile"),
            P("level", None, None, None, "tile"),
            P("level", None, None, None, None, "tile"),
            P("level", None, None, None, None, "tile"),
            P("tile", None),
            P("tile", None),
            P("tile", None),
            P("tile", None),
            P("tile", None),
        ),
        out_specs=P("level", None, None, None, None, "tile"),
        check_vma=False,
    )
```

```python
import functools

import jax
import jax.numpy as jnp
import numpy as np
from jax import lax
from jax.experimental import pallas as pl
from jax.experimental.pallas import tpu as pltpu
from jax.sharding import PartitionSpec as P

NP = 8
TSTEPS = 3
FCAP = 8


step_size = 0.02
penalty = 2.5
metric = 0.1
lift_factor = 2.8
weight_back = -1.0 / 12.0
weight_here = 8.0 / 12.0
weight_next = 5.0 / 12.0


def shifted(block, axis, distance):
    devices = range(lax.axis_size(axis))
    route = [(i - distance, i) for i in devices if i - distance in devices]
    return lax.ppermute(block, axis, route)


def lobatto_points():
    degree = NP - 1
    points = np.cos(np.pi * np.arange(degree + 1) / degree)
    table = np.zeros((degree + 1, degree + 1))
    for sweep in range(60):
        table[:, 0] = 1.0
        table[:, 1] = points
        for order in range(2, degree + 1):
            table[:, order] = (
                (2 * order - 1) * points * table[:, order - 1] - (order - 1) * table[:, order - 2]
            ) / order
        points = points - (points * table[:, degree] - table[:, degree - 1]) / (
            (degree + 1) * table[:, degree]
        )
    table[:, 0] = 1.0
    table[:, 1] = points
    for order in range(2, degree + 1):
        table[:, order] = (
            (2 * order - 1) * points * table[:, order - 1] - (order - 1) * table[:, order - 2]
        ) / order
    return (points[::-1], table[::-1, degree])


def derivative_numbers():
    degree = NP - 1
    points, values = lobatto_points()
    identity = np.eye(NP)
    spread = points[:, None] - points[None, :] + identity
    table = values[:, None] / values[None, :] / spread
    table = table * (1.0 - identity)
    table[0, 0] = -degree * (degree + 1) / 4.0
    table[degree, degree] = degree * (degree + 1) / 4.0
    return np.asarray(table, dtype=np.float32)

NV = 5
NODES = NP * NP
ROWS = NV * NODES
SIZE = NV * NP * NODES
CELLS = NP * NODES
STEPS = 8
SCALE = 1.0 / (TSTEPS * step_size)


def primitive(w):
    inverse = 1.0 / w[0]
    velocity = [w[c] * inverse for c in (1, 2, 3)]
    pressure = 0.4 * (w[4] - 0.5 * (w[1] * velocity[0] + w[2] * velocity[1] + w[3] * velocity[2]))
    return velocity, pressure


def flux(w, velocity, pressure, direction):
    carried = w[1 + direction]
    parts = [carried]
    for column in range(3):
        product = carried * velocity[column]
        if column == direction:
            product = product + pressure
        parts.append(product)
    parts.append((w[4] + pressure) * velocity[direction])
    return parts


def pieces_of(x):
    high = x.astype(jnp.bfloat16)
    rest = x - high.astype(jnp.float32)
    middle = rest.astype(jnp.bfloat16)
    low = (rest - middle.astype(jnp.float32)).astype(jnp.bfloat16)
    return [high, middle, low]


def face_rows(which):
    direction, end = which // 2, (NP - 1) * (which % 2)
    return direction, end


def trace_rows(ref, which, v):
    direction, end = face_rows(which)
    base = v * NP * NODES
    if direction == 0:
        return ref[pl.ds(base + end * NODES, NODES), :]
    if direction == 1:
        return jnp.concatenate(
            [ref[pl.ds(base + i * NODES + end * NP, NP), :] for i in range(NP)], axis=0
        )
    return ref[pl.ds(base + end, NODES, stride=NP), :]


def gather_traces(state, masks, turn, turned):
    width = state.shape[1]
    for which in range(6):
        lanes = pl.ds(which * width, width)
        mask = [jnp.broadcast_to(masks[o : o + 1, lanes], (NODES, width)) for o in range(4)]
        for v in range(NV):
            for at, piece in enumerate(pieces_of(trace_rows(state, which, v))):
                wide = piece.astype(jnp.float32)
                stacked = jnp.concatenate([(wide * m).astype(jnp.bfloat16) for m in mask], axis=0)
                out = jnp.dot(turn[...], stacked, preferred_element_type=jnp.float32)
                turned[at, pl.ds(v * NODES, NODES), lanes] = out.astype(jnp.bfloat16)


def outgoing_of(turned, send):
    outgoing = None
    for at in range(3):
        leave = lax.dot_general(
            send[...], turned[at], (((1,), (1,)), ((), ())), preferred_element_type=jnp.float32
        )
        outgoing = leave if outgoing is None else outgoing + leave
    return outgoing


def inner_of(turned, inner):
    total = None
    for at in range(3):
        part = jnp.dot(turned[at], inner[...], preferred_element_type=jnp.float32)
        total = part if total is None else total + part
    return total


def outer_of(arrived, place):
    total = None
    for piece in pieces_of(arrived):
        part = lax.dot_general(
            piece, place[...], (((0,), (0,)), ((), ())), preferred_element_type=jnp.float32
        )
        total = part if total is None else total + part
    return total


def volume_of(state, rolled, rate):
    numbers = derivative_numbers()

    def derived(fields):
        even = [fields[index] + fields[NP - 1 - index] for index in range(NP // 2)]
        odd = [fields[index] - fields[NP - 1 - index] for index in range(NP // 2)]
        results = [None] * NP
        for target in range(NP // 2):
            near = None
            far = None
            for index in range(NP // 2):
                here = float(numbers[target, index])
                there = float(numbers[target, NP - 1 - index])
                one = (-0.5 * metric * (here + there)) * even[index]
                two = (-0.5 * metric * (here - there)) * odd[index]
                near = one if near is None else near + one
                far = two if far is None else far + two
            results[target] = far + near
            results[NP - 1 - target] = far - near
        return results

    def at(v, i, j):
        return pl.ds(pl.multiple_of(v * NP * NODES + i * NODES + j * NP, NP), NP)

    def along_first(j, carry):
        across = [[None] * NP for v in range(NV)]
        down = [[None] * NP for v in range(NV)]
        for i in range(NP):
            w = [state[at(v, i, j), :] for v in range(NV)]
            velocity, pressure = primitive(w)
            for v, part in enumerate(flux(w, velocity, pressure, 0)):
                across[v][i] = part
            for v, part in enumerate(flux(w, velocity, pressure, 2)):
                total = rolled[0] * part
                for shift in range(1, NP):
                    total = total + rolled[shift] * pltpu.roll(part, NP - shift, 0)
                down[v][i] = total
        for v in range(NV):
            for i, part in enumerate(derived(across[v])):
                rate[at(v, i, j), :] = part + down[v][i]
        return carry

    def along_second(i, carry):
        across = [[None] * NP for v in range(NV)]
        for j in range(NP):
            w = [state[at(v, i, j), :] for v in range(NV)]
            velocity, pressure = primitive(w)
            for v, part in enumerate(flux(w, velocity, pressure, 1)):
                across[v][j] = part
        for v in range(NV):
            for j, part in enumerate(derived(across[v])):
                rate[at(v, i, j), :] = rate[at(v, i, j), :] + part
        return carry

    lax.fori_loop(0, NP, along_first, 0)
    lax.fori_loop(0, NP, along_second, 0)


def lift_faces(state, view, rate):
    width = state.shape[1]
    for which in range(6):
        direction, end = face_rows(which)
        normal = 2.0 * (which % 2) - 1.0
        lanes = pl.ds(which * width, width)

        def lift(row, carry):
            def rows(v):
                base = v * NP * NODES
                if direction == 0:
                    return pl.ds(pl.multiple_of(base + end * NODES + row * NP, NP), NP)
                if direction == 1:
                    return pl.ds(pl.multiple_of(base + row * NODES + end * NP, NP), NP)
                return pl.ds(base + row * NODES + end, NP, stride=NP)

            own = [state[rows(v), :] for v in range(NV)]
            far = [
                view[pl.ds(pl.multiple_of(v * NODES + row * NP, NP), NP), lanes]
                for v in range(NV)
            ]
            own_flux = flux(own, *primitive(own), direction)
            far_flux = flux(far, *primitive(far), direction)
            for v in range(NV):
                jump = (0.5 * normal) * (far_flux[v] - own_flux[v]) - (0.5 * penalty) * (
                    far[v] - own[v]
                )
                rate[rows(v), :] = rate[rows(v), :] - lift_factor * jump
            return carry

        lax.fori_loop(0, NP, lift, 0)


VMEM = pl.BlockSpec(memory_space=pltpu.VMEM)


def rate_kernel(count, *refs):
    states, refs = refs[:count], refs[count:]
    masks, turn, inner, send, place, rolled = refs[:6]
    rates, refs = refs[6 : 6 + count], refs[6 + count :]
    turned, views, buffer, landed, send_sem, recv_sem = refs
    tiles = lax.axis_size("tile")
    me = lax.axis_index("tile")
    barrier = pltpu.get_barrier_semaphore()

    def peer(offset):
        return {"tile": lax.rem(me + offset, tiles)}

    def copy(offset):
        return pltpu.make_async_remote_copy(
            src_ref=buffer.at[lax.rem(me + offset, tiles)],
            dst_ref=landed.at[me],
            send_sem=send_sem.at[offset],
            recv_sem=recv_sem.at[offset],
            device_id=peer(offset),
            device_id_type=pl.DeviceIdType.MESH,
        )

    def greet(offset, carry):
        pl.semaphore_signal(
            barrier, inc=1, device_id=peer(offset), device_id_type=pl.DeviceIdType.MESH
        )
        return carry

    def begin(offset, carry):
        copy(offset).start()
        return carry

    def finish(offset, carry):
        copy(offset).wait()
        return carry

    lax.fori_loop(1, tiles, greet, 0)
    for at in range(count):
        gather_traces(states[at], masks, turn, turned.at[at])
        leave = outgoing_of(turned.at[at], send)
        buffer[:, at * FCAP : (at + 1) * FCAP, :] = leave.reshape(tiles, FCAP, ROWS)
    pl.semaphore_wait(barrier, tiles - 1)
    lax.fori_loop(1, tiles, begin, 0)
    landed[me] = jnp.zeros(landed.shape[1:], jnp.float32)
    for at in range(count):
        views[at] = inner_of(turned.at[at], inner)
        volume_of(states[at], rolled, rates[at])
    lax.fori_loop(1, tiles, finish, 0)
    for at in range(count):
        arrived = landed[:, at * FCAP : (at + 1) * FCAP, :].reshape(tiles * FCAP, ROWS)
        views[at] = views[at] + outer_of(arrived, place)
        lift_faces(states[at], views.at[at], rates[at])


def rates_of(states, tables):
    tiles = lax.axis_size("tile")
    count = len(states)
    slots = tables[0].shape[1]
    like = jax.ShapeDtypeStruct(states[0].shape, jnp.float32)
    return pl.pallas_call(
        functools.partial(rate_kernel, count),
        out_shape=[like] * count,
        in_specs=[VMEM] * (count + len(tables)),
        out_specs=[VMEM] * count,
        scratch_shapes=[
            pltpu.VMEM((count, 3, ROWS, slots), jnp.bfloat16),
            pltpu.VMEM((count, ROWS, slots), jnp.float32),
            pltpu.VMEM((tiles, count * FCAP, ROWS), jnp.float32),
            pltpu.VMEM((tiles, count * FCAP, ROWS), jnp.float32),
            pltpu.SemaphoreType.DMA((tiles,)),
            pltpu.SemaphoreType.DMA((tiles,)),
        ],
        compiler_params=pltpu.CompilerParams(
            collective_id=count - 1, has_side_effects=True, vmem_limit_bytes=40 << 20
        ),
    )(*states, *tables)


def pieces_pair(x):
    high = x.astype(jnp.bfloat16)
    return high, (x - high.astype(jnp.float32)).astype(jnp.bfloat16)


def fluxes(w):
    inverse = 1.0 / w[0]
    velocity = [w[c] * inverse for c in (1, 2, 3)]
    product = {}
    for a in range(3):
        for b in range(a, 3):
            product[a, b] = product[b, a] = w[1 + a] * velocity[b]
    pressure = 0.4 * (w[4] - 0.5 * (product[0, 0] + product[1, 1] + product[2, 2]))
    total = w[4] + pressure
    return [
        [w[1 + d]]
        + [product[d, c] + pressure if c == d else product[d, c] for c in range(3)]
        + [total * velocity[d]]
        for d in range(3)
    ]


def derived(fields):
    numbers = derivative_numbers()
    even = [fields[index] + fields[NP - 1 - index] for index in range(NP // 2)]
    odd = [fields[index] - fields[NP - 1 - index] for index in range(NP // 2)]
    results = [None] * NP
    for target in range(NP // 2):
        near = None
        far = None
        for index in range(NP // 2):
            here = float(numbers[target, index])
            there = float(numbers[target, NP - 1 - index])
            one = (-0.5 * metric * (here + there)) * even[index]
            two = (-0.5 * metric * (here - there)) * odd[index]
            near = one if near is None else near + one
            far = two if far is None else far + two
        results[target] = far + near
        results[NP - 1 - target] = far - near
    return results


GROUP = 2 * NODES


def block_numbers():
    whole = np.kron(np.eye(GROUP // NP), -metric * derivative_numbers()).astype(np.float32)
    high = whole.astype(jnp.bfloat16)
    low = (whole - high.astype(np.float32)).astype(jnp.bfloat16)
    return np.concatenate([high, low, high], axis=1)


def spread_traces(state, spread, variables=range(NV)):
    width = state.shape[1]
    for which in range(6):
        lanes = pl.ds(which * width, width)
        for v in variables:
            high, low = pieces_pair(trace_rows(state, which, v))
            spread[pl.ds(v * NODES, NODES), lanes] = high
            spread[pl.ds(ROWS + v * NODES, NODES), lanes] = low


def node_rows(v, i, j, count=NP):
    return pl.ds(v * NP * NODES + i * NODES + j * NP, count)


def planes_and_views(state, spread, inner, flow, high, low, rate, view):
    width = state.shape[1]
    for i in range(NP):
        across = [[None] * NP for v in range(NV)]
        for j in range(0, NP, 2):
            thirds = [None, None]
            for half in range(2):
                w = [state[node_rows(v, i, j + half), :] for v in range(NV)]
                one, two, thirds[half] = fluxes(w)
                for v in range(NV):
                    across[v][j + half] = two[v]
                    flow[node_rows(v, i, j + half), :] = one[v]
            for v in range(NV):
                both = jnp.concatenate([thirds[0][v], thirds[1][v]], axis=0)
                upper, lower = pieces_pair(both)
                high[node_rows(v, i, j, 2 * NP), :] = upper
                low[node_rows(v, i, j, 2 * NP), :] = lower
        for v in range(NV):
            for j, part in enumerate(derived(across[v])):
                rate[node_rows(v, i, j), :] = part
        if i % 2 == 0 and i < 6:
            both = jnp.dot(
                spread[...], inner[:, i * width : (i + 2) * width],
                preferred_element_type=jnp.float32,
            )
            both = both[:ROWS] + both[ROWS:]
            for half in range(2):
                view[pl.ds((i + half) * ROWS, ROWS), :] = both[:, half * width : (half + 1) * width]


def remaining_volume(flow, high, low, blocks, rate):
    width = flow.shape[1]
    many = GROUP // NODES
    for v in range(NV):
        down = [None] * NP
        for i in range(0, NP // 2, many):

            def pair(ref):
                sides = [ref[node_rows(v, at, 0, GROUP), :] for at in (i, i + NP // 2)]
                return jnp.concatenate(sides, axis=1)

            upper, lower = pair(high), pair(low)
            both = jnp.dot(
                blocks[...],
                jnp.concatenate([upper, upper, lower], axis=0),
                preferred_element_type=jnp.float32,
            )
            for at in range(many):
                part = both[at * NODES : (at + 1) * NODES, :]
                down[i + at], down[i + at + NP // 2] = part[:, :width], part[:, width:]
        for j in range(NP):
            parts = derived([flow[node_rows(v, i, j), :] for i in range(NP)])
            for i, part in enumerate(parts):
                rows = node_rows(v, i, j)
                rate[rows, :] = rate[rows, :] + part + down[i][j * NP : (j + 1) * NP, :]


def lift_all(state, view, traces, place, orient, rate):
    width = state.shape[1]
    upper, lower = pieces_pair(traces.T)
    sides = jnp.concatenate([upper, lower], axis=0)
    outer = jnp.dot(sides, place[...], preferred_element_type=jnp.float32)
    outer = outer[:ROWS] + outer[ROWS:]
    for which in range(6):
        rows = pl.ds(which * ROWS, ROWS)
        view[rows, :] = view[rows, :] + outer[:, which * width : (which + 1) * width]
    ahead = lax.broadcasted_iota(jnp.int32, (NP, width), 0)
    for which in range(6):
        direction, end = face_rows(which)
        normal = 2.0 * (which % 2) - 1.0
        lanes = pl.ds(which * width, width)
        orients = jnp.broadcast_to(orient[0:1, lanes], (NP, width))
        crossed = (orients & 1) == 1
        turned = orients >= 2
        order = jnp.where(turned, NP - 1 - ahead, ahead)

        def rows_of(v, row):
            base = v * NP * NODES
            if direction == 0:
                return pl.ds(base + end * NODES + row * NP, NP)
            if direction == 1:
                return pl.ds(base + row * NODES + end * NP, NP)
            return pl.ds(base + row * NODES + end, NP, stride=NP)

        for near in range(NP // 2):
            pair = [near, NP - 1 - near]
            far = [[], []]
            for v in range(NV):
                base = which * ROWS + v * NODES
                seen = [
                    jnp.where(
                        crossed,
                        view[pl.ds(base + row, NP, stride=NP), :],
                        view[pl.ds(base + row * NP, NP), :],
                    )
                    for row in pair
                ]
                for half in range(2):
                    picked = jnp.where(turned, seen[1 - half], seen[half])
                    far[half].append(
                        jnp.take_along_axis(picked, order, axis=0, mode="promise_in_bounds")
                    )
            for half in range(2):
                rows = [rows_of(v, pair[half]) for v in range(NV)]
                own = [state[rows[v], :] for v in range(NV)]
                own_flux = flux(own, *primitive(own), direction)
                far_flux = flux(far[half], *primitive(far[half]), direction)
                for v in range(NV):
                    jump = (0.5 * normal) * (far_flux[v] - own_flux[v]) - (0.5 * penalty) * (
                        far[half][v] - own[v]
                    )
                    rate[rows[v], :] = rate[rows[v], :] - lift_factor * jump


def table_rows(ref, fill):
    row = ref[...].astype(jnp.float32)
    extra = -row.shape[1] % 128
    if extra > 0:
        row = jnp.concatenate([row, jnp.full((1, extra), fill, jnp.float32)], axis=1)
    return row


def fill_tables(peers, matches, slots, partner, inner, send, place):
    faces = partner.shape[1]
    pack = 16

    def some(at, carry):
        base = pl.multiple_of(at * pack, pack)
        ids = lax.broadcasted_iota(jnp.int32, (pack, faces), 0) + base
        lane = lax.broadcasted_iota(jnp.int32, (pack, faces), 1)
        mate = jnp.broadcast_to(partner[...], (pack, faces))
        hit = jnp.where((ids == mate) & (mate != lane), 1.0, 0.0)
        inner[pl.ds(base, pack), :] = hit.astype(jnp.bfloat16)
        return carry

    lax.fori_loop(0, faces // pack, some, 0)
    peer = table_rows(peers, -1.0)
    match = table_rows(matches, -1.0)
    slot = table_rows(slots, -1.0)
    count = peer.shape[1]
    square = (count, count)
    peer_across = jnp.broadcast_to(peer, square)
    match_across = jnp.broadcast_to(match, square)
    same = peer_across.T == peer_across
    lower = match_across.T < match_across
    sooner = lax.broadcasted_iota(jnp.int32, square, 0) < lax.broadcasted_iota(jnp.int32, square, 1)
    slot_of = lax.broadcasted_iota(jnp.int32, (faces, count), 0).astype(jnp.float32)
    at_slot = jnp.where(slot_of == jnp.broadcast_to(slot, (faces, count)), 1.0, 0.0)
    at_slot = at_slot.astype(jnp.bfloat16)
    places = send.shape[0]
    spots = lax.broadcasted_iota(jnp.int32, (places, count), 0).astype(jnp.float32)
    for ahead, table in ((lower, send), (sooner, place)):
        rank = jnp.sum(jnp.where(same & ahead, 1.0, 0.0), axis=0, keepdims=True)
        spot = jnp.broadcast_to(peer * FCAP + rank, (places, count))
        onehot = jnp.where(spots == spot, 1.0, 0.0).astype(jnp.bfloat16)
        routed = lax.dot_general(
            onehot, at_slot, (((1,), (1,)), ((), ())), preferred_element_type=jnp.float32
        )
        table[...] = routed.astype(jnp.bfloat16)


def window_kernel(*refs):
    fields, refs = refs[:5], refs[5:]
    indices, refs = refs[:6], refs[6:]
    out, refs = refs[0], refs[1:]
    states, rates, older, old, refs = refs[0], refs[1], refs[2], refs[3], refs[4:]
    held, refs = refs[:6], refs[6:]
    inner, send, place, spread, flow, high, low, view, refs = *refs[:8], refs[8:]
    parcels, landings, refs = refs[:2], refs[2:4], refs[4:]
    buffer, traces, send_sem, recv_sem, load_sem, table_sem, pass_send, pass_recv = refs
    peers, matches, slots, partner, orient, blocks = held
    tiles = lax.axis_size("tile")
    me = lax.axis_index("tile")
    level = lax.axis_index("level")
    base_level = level == 0
    upper = (level > 0).astype(jnp.float32)
    other = {"level": 1 - level}
    barrier = pltpu.get_barrier_semaphore()
    parts = [
        (fields[0], 0, CELLS),
        (fields[1], CELLS, 3 * CELLS),
        (fields[2], 4 * CELLS, CELLS),
    ]

    def peer(offset):
        return {"tile": lax.rem(me + offset, tiles)}

    def swap(stage, offset):
        return pltpu.make_async_remote_copy(
            src_ref=buffer.at[stage, lax.rem(me + offset, tiles)],
            dst_ref=traces.at[stage, me],
            send_sem=send_sem.at[stage, offset],
            recv_sem=recv_sem.at[stage, offset],
            device_id=peer(offset),
            device_id_type=pl.DeviceIdType.MESH,
        )

    def portion(at, offset):
        return pltpu.make_async_remote_copy(
            src_ref=parcels[at].at[lax.rem(me + offset, tiles)],
            dst_ref=landings[at].at[me],
            send_sem=send_sem.at[TSTEPS + at, offset],
            recv_sem=recv_sem.at[TSTEPS + at, offset],
            device_id=peer(offset),
            device_id_type=pl.DeviceIdType.MESH,
        )

    def handed(at):
        ref, base, count = parts[at]
        return pltpu.make_async_remote_copy(
            src_ref=ref,
            dst_ref=states.at[2, pl.ds(base, count), :],
            send_sem=pass_send.at[at],
            recv_sem=pass_recv.at[at],
            device_id=other,
            device_id_type=pl.DeviceIdType.MESH,
        )

    def forwarded(stage):
        return pltpu.make_async_remote_copy(
            src_ref=traces.at[stage],
            dst_ref=traces.at[TSTEPS + stage],
            send_sem=pass_send.at[3 + stage],
            recv_sem=pass_recv.at[3 + stage],
            device_id=other,
            device_id_type=pl.DeviceIdType.MESH,
        )

    def greet(offset, carry):
        pl.semaphore_signal(
            barrier, inc=1, device_id=peer(offset), device_id_type=pl.DeviceIdType.MESH
        )
        return carry

    pl.semaphore_signal(barrier, inc=1, device_id=other, device_id_type=pl.DeviceIdType.MESH)
    lax.fori_loop(1, tiles, greet, 0)
    tables = [
        pltpu.make_async_copy(ref, kept, table_sem.at[at])
        for at, (ref, kept) in enumerate(zip(indices, held))
    ]
    loads = [
        pltpu.make_async_copy(ref, states.at[0, pl.ds(base, count), :], load_sem.at[at])
        for at, (ref, base, count) in enumerate(parts)
    ]
    loads.append(pltpu.make_async_copy(fields[3], older, load_sem.at[3]))
    loads.append(pltpu.make_async_copy(fields[4], old, load_sem.at[4]))
    for load in tables + loads:
        load.start()
    pl.semaphore_wait(barrier, tiles)

    @pl.when(base_level)
    def _():
        for at in range(3):
            handed(at).start()

    for load in tables:
        load.wait()
    fill_tables(peers, matches, slots, partner, inner, send, place)
    for stage in range(TSTEPS):
        traces[stage, me] = jnp.zeros(traces.shape[2:], jnp.float32)
    for landing in landings:
        landing[me] = jnp.zeros(landing.shape[1:], jnp.float32)
    for load in loads:
        load.wait()

    def arrive(stage):
        def finish(offset, carry):
            swap(stage, offset).wait()
            return carry

        lax.fori_loop(1, tiles, finish, 0)

    def sweep(work):
        rows = SIZE // 8

        def chunk(at, carry):
            work(pl.ds(pl.multiple_of(at * rows, rows), rows))
            return carry

        lax.fori_loop(0, 8, chunk, 0)

    def share_out(at, state, variables):
        spread_traces(state, spread, variables)
        leave = None
        for half in range(2):
            rows = pl.ds(half * ROWS + variables[0] * NODES, len(variables) * NODES)
            part = lax.dot_general(
                send[...], spread[rows, :], (((1,), (1,)), ((), ())),
                preferred_element_type=jnp.float32,
            )
            leave = part if leave is None else leave + part
        parcels[at][...] = leave.reshape(parcels[at].shape)

        def begin(offset, carry):
            portion(at, offset).start()
            return carry

        lax.fori_loop(1, tiles, begin, 0)

    def collect(at):
        def finish(offset, carry):
            portion(at, offset).wait()
            return carry

        lax.fori_loop(1, tiles, finish, 0)

    def step(t, carry):
        def on(base, at):
            return pl.when((level == 0) & (t == at) if base else (level > 0) & (t == at))

        state, rate = states.at[t], rates.at[t]
        stage = jnp.where(t <= 1, t, 2)
        leaving = jnp.where(base_level, t <= 2, (t <= 1) | (t == 4))
        lasting = jnp.where(base_level, t <= 2, (t != 1) & (t != 4))

        @on(False, 2)
        def _():
            for at in range(2):
                handed(at).wait_recv()
            share_out(0, state, range(NV - 1))
            handed(2).wait_recv()
            share_out(1, state, range(NV - 1, NV))

        @pl.when((leaving | lasting) & (base_level | (t != 2)))
        def _():
            spread_traces(state, spread)

        @pl.when(leaving)
        def _():
            leave = lax.dot_general(
                send[...], spread[...], (((1,), (1,)), ((), ())), preferred_element_type=jnp.float32
            )
            leave = leave[:, :ROWS] + leave[:, ROWS:]
            buffer[stage] = leave.reshape(tiles, FCAP, ROWS)

            def begin(offset, carry):
                swap(stage, offset).start()
                return carry

            lax.fori_loop(1, tiles, begin, 0)

        @pl.when(lasting)
        def _():
            planes_and_views(state, spread, inner, flow, high, low, rate, view)
            remaining_volume(flow, high, low, blocks, rate)

            @pl.when(base_level | (t == 0))
            def _():
                arrive(stage)

            @on(True, 2)
            def _():
                for at in range(3):
                    handed(at).wait_send()
                forwarded(1).start()
                forwarded(2).start()

            @on(False, 2)
            def _():
                for at in range(2):
                    collect(at)
                traces[TSTEPS] = jnp.concatenate(
                    [landing[...] for landing in landings], axis=2
                )

            @on(False, 3)
            def _():
                arrive(1)
                forwarded(1).wait_recv()

            @on(False, 6)
            def _():
                forwarded(2).wait_recv()

            @on(False, 7)
            def _():
                arrive(2)

            own = jnp.where(
                base_level | (t == 0),
                t,
                jnp.where(t == 3, 1, jnp.where(t == 7, 2, jnp.where(t == 2, 3, t - 1))),
            )
            mixed = (level > 0) & ((t == 3) | (t == 7))
            newer = jnp.where(mixed, jnp.where(t == 3, 4, 5), own)
            elder = jnp.where(mixed, newer - 1, own)
            share = jnp.where(mixed, weight_next, 0.0)
            seen = traces[own] + share * (traces[newer] - traces[elder])
            lift_all(state, view, seen.reshape(tiles * FCAP, ROWS), place, orient, rate)

        @pl.when(t == 0)
        def _():
            def work(rows):
                extra = weight_back * older[rows, :] + (weight_here - 1.0) * old[rows, :]
                states[1, rows, :] = states[0, rows, :] + step_size * (
                    rates[0, rows, :] + upper * extra
                )

            sweep(work)

        @on(True, 1)
        def _():
            def work(rows):
                states[2, rows, :] = states[1, rows, :] + step_size * rates[1, rows, :]

            sweep(work)

        @on(True, 2)
        def _():
            def work(rows):
                moved = states[2, rows, :] + step_size * rates[2, rows, :] - states[0, rows, :]
                out[rows, :] = moved * SCALE

            sweep(work)

        @on(False, 2)
        def _():
            def work(rows):
                below = step_size * rates[2, rows, :]
                states[3, rows, :] = states[1, rows, :] + weight_next * below
                states[5, rows, :] = states[2, rows, :] + below

            sweep(work)

        @on(False, 3)
        def _():
            def work(rows):
                states[4, rows, :] = states[3, rows, :] + step_size * (
                    rates[3, rows, :]
                    + weight_back * old[rows, :]
                    + (weight_here - 1.0) * rates[2, rows, :]
                )

            sweep(work)

        @on(False, 5)
        def _():
            def work(rows):
                below = step_size * rates[5, rows, :]
                states[7, rows, :] = states[4, rows, :] + weight_next * below
                states[6, rows, :] = states[5, rows, :] + below

            sweep(work)

        @on(False, 7)
        def _():
            def work(rows):
                change = (
                    rates[7, rows, :]
                    + weight_back * rates[2, rows, :]
                    + (weight_here - 1.0) * rates[5, rows, :]
                    + weight_next * rates[6, rows, :]
                )
                moved = states[7, rows, :] + step_size * change - states[0, rows, :]
                out[rows, :] = moved * SCALE

            sweep(work)

        return carry

    lax.fori_loop(0, STEPS, step, 0)

    @pl.when(base_level)
    def _():
        for stage in range(1, TSTEPS):
            forwarded(stage).wait_send()


def window_of(fields, indices):
    tiles = lax.axis_size("tile")
    width = fields[0].shape[1]
    faces = indices[3].shape[1]
    full = (SIZE, width)
    f32, bf16 = jnp.float32, jnp.bfloat16
    operands = [*fields, *indices, jnp.asarray(block_numbers())]
    operands = [pltpu.with_memory_space_constraint(x, pltpu.HBM) for x in operands]
    return pl.pallas_call(
        window_kernel,
        out_shape=jax.ShapeDtypeStruct(full, f32),
        in_specs=[pl.BlockSpec(memory_space=pl.ANY)] * len(operands),
        out_specs=VMEM,
        scratch_shapes=[
            pltpu.VMEM((STEPS,) + full, f32),
            pltpu.VMEM((STEPS,) + full, f32),
            pltpu.VMEM(full, f32),
            pltpu.VMEM(full, f32),
            *[pltpu.VMEM(x.shape, x.dtype) for x in operands[5:]],
            pltpu.VMEM((faces, faces), bf16),
            pltpu.VMEM((tiles * FCAP, faces), bf16),
            pltpu.VMEM((tiles * FCAP, faces), bf16),
            pltpu.VMEM((2 * ROWS, faces), bf16),
            pltpu.VMEM(full, f32),
            pltpu.VMEM(full, bf16),
            pltpu.VMEM(full, bf16),
            pltpu.VMEM((6 * ROWS, width), f32),
            *[pltpu.VMEM((tiles, FCAP, many * NODES), f32) for many in (NV - 1, 1, NV - 1, 1)],
            pltpu.VMEM((TSTEPS, tiles, FCAP, ROWS), f32),
            pltpu.VMEM((2 * TSTEPS, tiles, FCAP, ROWS), f32),
            pltpu.SemaphoreType.DMA((TSTEPS + 2, tiles)),
            pltpu.SemaphoreType.DMA((TSTEPS + 2, tiles)),
            pltpu.SemaphoreType.DMA((5,)),
            pltpu.SemaphoreType.DMA((6,)),
            pltpu.SemaphoreType.DMA((6,)),
            pltpu.SemaphoreType.DMA((6,)),
        ],
        compiler_params=pltpu.CompilerParams(
            collective_id=2, has_side_effects=True, vmem_limit_bytes=44 << 20
        ),
    )(*operands)


def turning():
    nodes = np.arange(NODES)
    blocks = []
    for orient in range(4):
        source = nodes.reshape(NP, NP)
        if orient >= 2:
            source = source[::-1, ::-1]
        if orient % 2 == 1:
            source = source.T
        block = np.zeros((NODES, NODES), np.float32)
        block[nodes, source.reshape(-1)] = 1.0
        blocks.append(block)
    return np.concatenate(blocks, axis=1)


def body(
    density,
    momentum,
    energy,
    rhs_older,
    rhs_old,
    peer_tile,
    peer_index,
    boundary_slot,
    face_partner,
    face_orient,
):
    width = density.shape[-1]
    if lax.axis_size("level") == 2:
        fields = [density, momentum, energy, rhs_older, rhs_old]
        indices = [peer_tile, peer_index, boundary_slot, face_partner, face_orient]
        result = window_of([field.reshape(-1, width) for field in fields], indices)
        return result.reshape(rhs_old.shape)
    start = jnp.concatenate(
        [
            density.reshape(-1, width),
            momentum.reshape(-1, width),
            energy.reshape(-1, width),
        ],
        axis=0,
    )
    level = lax.axis_index("level")
    tiles = lax.axis_size("tile")
    peers = peer_tile[0]
    matches = peer_index[0]
    slots = boundary_slot[0]
    partner = face_partner[0]
    orient = face_orient[0]
    count = peers.shape[0]
    faces = partner.shape[0]
    same_peer = peers[:, None] == peers[None, :]
    listing = jnp.arange(count, dtype=jnp.int32)
    send_rank = jnp.sum(same_peer & (matches[None, :] < matches[:, None]), axis=1, dtype=jnp.int32)
    recv_rank = jnp.sum(same_peer & (listing[None, :] < listing[:, None]), axis=1, dtype=jnp.int32)
    places = jnp.arange(tiles * FCAP, dtype=jnp.int32)
    ids = jnp.arange(faces, dtype=jnp.int32)
    exact = jnp.bfloat16
    at_slot = (slots[:, None] == ids[None, :]).astype(exact)

    def routing(rank):
        onehot = (places[:, None] == (peers * FCAP + rank)[None, :]).astype(exact)
        return jnp.dot(onehot, at_slot, preferred_element_type=jnp.float32).astype(exact)

    send = routing(send_rank)
    place = routing(recv_rank)
    inner = ((ids[:, None] == partner[None, :]) & (partner != ids)[None, :]).astype(exact)
    masks = (orient[None, :] == jnp.arange(8, dtype=jnp.int32)[:, None]).astype(jnp.float32)
    turn = jnp.asarray(turning(), exact)
    numbers = derivative_numbers()
    diagonals = np.stack(
        [
            np.stack([-metric * numbers[k, (k + shift) % NP] for k in range(NP)])
            for shift in range(NP)
        ]
    ).astype(np.float32)
    rolled = jnp.broadcast_to(jnp.asarray(diagonals)[:, :, None], (NP, NP, width))

    tables = (masks, turn, inner, send, place, rolled)

    def rates(states):
        return rates_of(states, tables)

    older = rhs_older.reshape(-1, width)
    old = rhs_old.reshape(-1, width)

    def advance(state, own_rate, older, old, below):
        corrected = (
            state
            + step_size * (own_rate - old)
            + step_size * (weight_back * older + weight_here * old + weight_next * below)
        )
        return jnp.where(level == 0, state + step_size * own_rate, corrected)

    state = start
    for repeat in range(TSTEPS):
        own_rate = rates([state])[0]
        below = shifted(own_rate, "level", 1)
        state = advance(state, own_rate, older, old, below)
        older = old
        old = below
    return ((state - start) / (TSTEPS * step_size)).reshape(rhs_old.shape)


def solution(mesh):
    return jax.shard_map(
        body,
        mesh=mesh,
        in_specs=(
            P("level", None, None, None, "tile"),
            P("level", None, None, None, None, "tile"),
            P("level", None, None, None, "tile"),
            P("level", None, None, None, None, "tile"),
            P("level", None, None, None, None, "tile"),
            P("tile", None),
            P("tile", None),
            P("tile", None),
            P("tile", None),
            P("tile", None),
        ),
        out_specs=P("level", None, None, None, None, "tile"),
        check_vma=False,
    )
```

```python
import functools

import jax
import jax.numpy as jnp
import numpy as np
from jax import lax
from jax.experimental import pallas as pl
from jax.experimental.pallas import tpu as pltpu
from jax.sharding import PartitionSpec as P

NP = 8
TSTEPS = 3
FCAP = 8


step_size = 0.02
penalty = 2.5
metric = 0.1
lift_factor = 2.8
weight_back = -1.0 / 12.0
weight_here = 8.0 / 12.0
weight_next = 5.0 / 12.0


def shifted(block, axis, distance):
    devices = range(lax.axis_size(axis))
    route = [(i - distance, i) for i in devices if i - distance in devices]
    return lax.ppermute(block, axis, route)


def lobatto_points():
    degree = NP - 1
    points = np.cos(np.pi * np.arange(degree + 1) / degree)
    table = np.zeros((degree + 1, degree + 1))
    for sweep in range(60):
        table[:, 0] = 1.0
        table[:, 1] = points
        for order in range(2, degree + 1):
            table[:, order] = (
                (2 * order - 1) * points * table[:, order - 1] - (order - 1) * table[:, order - 2]
            ) / order
        points = points - (points * table[:, degree] - table[:, degree - 1]) / (
            (degree + 1) * table[:, degree]
        )
    table[:, 0] = 1.0
    table[:, 1] = points
    for order in range(2, degree + 1):
        table[:, order] = (
            (2 * order - 1) * points * table[:, order - 1] - (order - 1) * table[:, order - 2]
        ) / order
    return (points[::-1], table[::-1, degree])


def derivative_numbers():
    degree = NP - 1
    points, values = lobatto_points()
    identity = np.eye(NP)
    spread = points[:, None] - points[None, :] + identity
    table = values[:, None] / values[None, :] / spread
    table = table * (1.0 - identity)
    table[0, 0] = -degree * (degree + 1) / 4.0
    table[degree, degree] = degree * (degree + 1) / 4.0
    return np.asarray(table, dtype=np.float32)

NV = 5
NODES = NP * NP
ROWS = NV * NODES
SIZE = NV * NP * NODES
CELLS = NP * NODES
STEPS = 8
SCALE = 1.0 / (TSTEPS * step_size)


def primitive(w):
    inverse = 1.0 / w[0]
    velocity = [w[c] * inverse for c in (1, 2, 3)]
    pressure = 0.4 * (w[4] - 0.5 * (w[1] * velocity[0] + w[2] * velocity[1] + w[3] * velocity[2]))
    return velocity, pressure


def flux(w, velocity, pressure, direction):
    carried = w[1 + direction]
    parts = [carried]
    for column in range(3):
        product = carried * velocity[column]
        if column == direction:
            product = product + pressure
        parts.append(product)
    parts.append((w[4] + pressure) * velocity[direction])
    return parts


def pieces_of(x):
    high = x.astype(jnp.bfloat16)
    rest = x - high.astype(jnp.float32)
    middle = rest.astype(jnp.bfloat16)
    low = (rest - middle.astype(jnp.float32)).astype(jnp.bfloat16)
    return [high, middle, low]


def face_rows(which):
    direction, end = which // 2, (NP - 1) * (which % 2)
    return direction, end


def trace_rows(ref, which, v):
    direction, end = face_rows(which)
    base = v * NP * NODES
    if direction == 0:
        return ref[pl.ds(base + end * NODES, NODES), :]
    if direction == 1:
        return jnp.concatenate(
            [ref[pl.ds(base + i * NODES + end * NP, NP), :] for i in range(NP)], axis=0
        )
    return ref[pl.ds(base + end, NODES, stride=NP), :]


def gather_traces(state, masks, turn, turned):
    width = state.shape[1]
    for which in range(6):
        lanes = pl.ds(which * width, width)
        mask = [jnp.broadcast_to(masks[o : o + 1, lanes], (NODES, width)) for o in range(4)]
        for v in range(NV):
            for at, piece in enumerate(pieces_of(trace_rows(state, which, v))):
                wide = piece.astype(jnp.float32)
                stacked = jnp.concatenate([(wide * m).astype(jnp.bfloat16) for m in mask], axis=0)
                out = jnp.dot(turn[...], stacked, preferred_element_type=jnp.float32)
                turned[at, pl.ds(v * NODES, NODES), lanes] = out.astype(jnp.bfloat16)


def outgoing_of(turned, send):
    outgoing = None
    for at in range(3):
        leave = lax.dot_general(
            send[...], turned[at], (((1,), (1,)), ((), ())), preferred_element_type=jnp.float32
        )
        outgoing = leave if outgoing is None else outgoing + leave
    return outgoing


def inner_of(turned, inner):
    total = None
    for at in range(3):
        part = jnp.dot(turned[at], inner[...], preferred_element_type=jnp.float32)
        total = part if total is None else total + part
    return total


def outer_of(arrived, place):
    total = None
    for piece in pieces_of(arrived):
        part = lax.dot_general(
            piece, place[...], (((0,), (0,)), ((), ())), preferred_element_type=jnp.float32
        )
        total = part if total is None else total + part
    return total


def volume_of(state, rolled, rate):
    numbers = derivative_numbers()

    def derived(fields):
        even = [fields[index] + fields[NP - 1 - index] for index in range(NP // 2)]
        odd = [fields[index] - fields[NP - 1 - index] for index in range(NP // 2)]
        results = [None] * NP
        for target in range(NP // 2):
            near = None
            far = None
            for index in range(NP // 2):
                here = float(numbers[target, index])
                there = float(numbers[target, NP - 1 - index])
                one = (-0.5 * metric * (here + there)) * even[index]
                two = (-0.5 * metric * (here - there)) * odd[index]
                near = one if near is None else near + one
                far = two if far is None else far + two
            results[target] = far + near
            results[NP - 1 - target] = far - near
        return results

    def at(v, i, j):
        return pl.ds(pl.multiple_of(v * NP * NODES + i * NODES + j * NP, NP), NP)

    def along_first(j, carry):
        across = [[None] * NP for v in range(NV)]
        down = [[None] * NP for v in range(NV)]
        for i in range(NP):
            w = [state[at(v, i, j), :] for v in range(NV)]
            velocity, pressure = primitive(w)
            for v, part in enumerate(flux(w, velocity, pressure, 0)):
                across[v][i] = part
            for v, part in enumerate(flux(w, velocity, pressure, 2)):
                total = rolled[0] * part
                for shift in range(1, NP):
                    total = total + rolled[shift] * pltpu.roll(part, NP - shift, 0)
                down[v][i] = total
        for v in range(NV):
            for i, part in enumerate(derived(across[v])):
                rate[at(v, i, j), :] = part + down[v][i]
        return carry

    def along_second(i, carry):
        across = [[None] * NP for v in range(NV)]
        for j in range(NP):
            w = [state[at(v, i, j), :] for v in range(NV)]
            velocity, pressure = primitive(w)
            for v, part in enumerate(flux(w, velocity, pressure, 1)):
                across[v][j] = part
        for v in range(NV):
            for j, part in enumerate(derived(across[v])):
                rate[at(v, i, j), :] = rate[at(v, i, j), :] + part
        return carry

    lax.fori_loop(0, NP, along_first, 0)
    lax.fori_loop(0, NP, along_second, 0)


def lift_faces(state, view, rate):
    width = state.shape[1]
    for which in range(6):
        direction, end = face_rows(which)
        normal = 2.0 * (which % 2) - 1.0
        lanes = pl.ds(which * width, width)

        def lift(row, carry):
            def rows(v):
                base = v * NP * NODES
                if direction == 0:
                    return pl.ds(pl.multiple_of(base + end * NODES + row * NP, NP), NP)
                if direction == 1:
                    return pl.ds(pl.multiple_of(base + row * NODES + end * NP, NP), NP)
                return pl.ds(base + row * NODES + end, NP, stride=NP)

            own = [state[rows(v), :] for v in range(NV)]
            far = [
                view[pl.ds(pl.multiple_of(v * NODES + row * NP, NP), NP), lanes]
                for v in range(NV)
            ]
            own_flux = flux(own, *primitive(own), direction)
            far_flux = flux(far, *primitive(far), direction)
            for v in range(NV):
                jump = (0.5 * normal) * (far_flux[v] - own_flux[v]) - (0.5 * penalty) * (
                    far[v] - own[v]
                )
                rate[rows(v), :] = rate[rows(v), :] - lift_factor * jump
            return carry

        lax.fori_loop(0, NP, lift, 0)


VMEM = pl.BlockSpec(memory_space=pltpu.VMEM)


def rate_kernel(count, *refs):
    states, refs = refs[:count], refs[count:]
    masks, turn, inner, send, place, rolled = refs[:6]
    rates, refs = refs[6 : 6 + count], refs[6 + count :]
    turned, views, buffer, landed, send_sem, recv_sem = refs
    tiles = lax.axis_size("tile")
    me = lax.axis_index("tile")
    barrier = pltpu.get_barrier_semaphore()

    def peer(offset):
        return {"tile": lax.rem(me + offset, tiles)}

    def copy(offset):
        return pltpu.make_async_remote_copy(
            src_ref=buffer.at[lax.rem(me + offset, tiles)],
            dst_ref=landed.at[me],
            send_sem=send_sem.at[offset],
            recv_sem=recv_sem.at[offset],
            device_id=peer(offset),
            device_id_type=pl.DeviceIdType.MESH,
        )

    def greet(offset, carry):
        pl.semaphore_signal(
            barrier, inc=1, device_id=peer(offset), device_id_type=pl.DeviceIdType.MESH
        )
        return carry

    def begin(offset, carry):
        copy(offset).start()
        return carry

    def finish(offset, carry):
        copy(offset).wait()
        return carry

    lax.fori_loop(1, tiles, greet, 0)
    for at in range(count):
        gather_traces(states[at], masks, turn, turned.at[at])
        leave = outgoing_of(turned.at[at], send)
        buffer[:, at * FCAP : (at + 1) * FCAP, :] = leave.reshape(tiles, FCAP, ROWS)
    pl.semaphore_wait(barrier, tiles - 1)
    lax.fori_loop(1, tiles, begin, 0)
    landed[me] = jnp.zeros(landed.shape[1:], jnp.float32)
    for at in range(count):
        views[at] = inner_of(turned.at[at], inner)
        volume_of(states[at], rolled, rates[at])
    lax.fori_loop(1, tiles, finish, 0)
    for at in range(count):
        arrived = landed[:, at * FCAP : (at + 1) * FCAP, :].reshape(tiles * FCAP, ROWS)
        views[at] = views[at] + outer_of(arrived, place)
        lift_faces(states[at], views.at[at], rates[at])


def rates_of(states, tables):
    tiles = lax.axis_size("tile")
    count = len(states)
    slots = tables[0].shape[1]
    like = jax.ShapeDtypeStruct(states[0].shape, jnp.float32)
    return pl.pallas_call(
        functools.partial(rate_kernel, count),
        out_shape=[like] * count,
        in_specs=[VMEM] * (count + len(tables)),
        out_specs=[VMEM] * count,
        scratch_shapes=[
            pltpu.VMEM((count, 3, ROWS, slots), jnp.bfloat16),
            pltpu.VMEM((count, ROWS, slots), jnp.float32),
            pltpu.VMEM((tiles, count * FCAP, ROWS), jnp.float32),
            pltpu.VMEM((tiles, count * FCAP, ROWS), jnp.float32),
            pltpu.SemaphoreType.DMA((tiles,)),
            pltpu.SemaphoreType.DMA((tiles,)),
        ],
        compiler_params=pltpu.CompilerParams(
            collective_id=count - 1, has_side_effects=True, vmem_limit_bytes=40 << 20
        ),
    )(*states, *tables)


def pieces_pair(x):
    high = x.astype(jnp.bfloat16)
    return high, (x - high.astype(jnp.float32)).astype(jnp.bfloat16)


def fluxes(w):
    inverse = 1.0 / w[0]
    velocity = [w[c] * inverse for c in (1, 2, 3)]
    product = {}
    for a in range(3):
        for b in range(a, 3):
            product[a, b] = product[b, a] = w[1 + a] * velocity[b]
    pressure = 0.4 * (w[4] - 0.5 * (product[0, 0] + product[1, 1] + product[2, 2]))
    total = w[4] + pressure
    return [
        [w[1 + d]]
        + [product[d, c] + pressure if c == d else product[d, c] for c in range(3)]
        + [total * velocity[d]]
        for d in range(3)
    ]


def derived(fields):
    numbers = derivative_numbers()
    count = NP // 2
    even = [fields[index] + fields[NP - 1 - index] for index in range(count)]
    odd = [fields[index] - fields[NP - 1 - index] for index in range(count)]
    against = [even[index] - even[count - 1] for index in range(count - 1)]
    results = [None] * NP
    for target in range(count):
        near = None
        far = None
        for index in range(count):
            here = float(numbers[target, index])
            there = float(numbers[target, NP - 1 - index])
            two = (-0.5 * metric * (here - there)) * odd[index]
            far = two if far is None else far + two
            if index < count - 1:
                one = (-0.5 * metric * (here + there)) * against[index]
                near = one if near is None else near + one
        results[target] = far + near
        results[NP - 1 - target] = far - near
    return results


GROUP = 2 * NODES


def block_numbers():
    whole = np.kron(np.eye(GROUP // NP), -metric * derivative_numbers()).astype(np.float32)
    high = whole.astype(jnp.bfloat16)
    low = (whole - high.astype(np.float32)).astype(jnp.bfloat16)
    return np.concatenate([high, low, high], axis=1)


def spread_traces(state, spread, variables=range(NV)):
    width = state.shape[1]
    for which in range(6):
        lanes = pl.ds(which * width, width)
        for v in variables:
            high, low = pieces_pair(trace_rows(state, which, v))
            spread[pl.ds(v * NODES, NODES), lanes] = high
            spread[pl.ds(ROWS + v * NODES, NODES), lanes] = low


def node_rows(v, i, j, count=NP):
    return pl.ds(v * NP * NODES + i * NODES + j * NP, count)


def planes_and_views(state, spread, inner, flow, high, low, rate, view):
    width = state.shape[1]
    for i in range(NP):
        across = [[None] * NP for v in range(NV)]
        for j in range(0, NP, 2):
            thirds = [None, None]
            for half in range(2):
                w = [state[node_rows(v, i, j + half), :] for v in range(NV)]
                one, two, thirds[half] = fluxes(w)
                for v in range(NV):
                    across[v][j + half] = two[v]
                    flow[node_rows(v, i, j + half), :] = one[v]
            for v in range(NV):
                both = jnp.concatenate([thirds[0][v], thirds[1][v]], axis=0)
                upper, lower = pieces_pair(both)
                high[node_rows(v, i, j, 2 * NP), :] = upper
                low[node_rows(v, i, j, 2 * NP), :] = lower
        for v in range(NV):
            for j, part in enumerate(derived(across[v])):
                rate[node_rows(v, i, j), :] = part
        if i % 2 == 0 and i < 6:
            both = jnp.dot(
                spread[...], inner[:, i * width : (i + 2) * width],
                preferred_element_type=jnp.float32,
            )
            both = both[:ROWS] + both[ROWS:]
            for half in range(2):
                view[pl.ds((i + half) * ROWS, ROWS), :] = both[:, half * width : (half + 1) * width]


def remaining_volume(flow, high, low, blocks, rate):
    width = flow.shape[1]
    many = GROUP // NODES
    for v in range(NV):
        down = [None] * NP
        for i in range(0, NP // 2, many):

            def pair(ref):
                sides = [ref[node_rows(v, at, 0, GROUP), :] for at in (i, i + NP // 2)]
                return jnp.concatenate(sides, axis=1)

            upper, lower = pair(high), pair(low)
            both = jnp.dot(
                blocks[...],
                jnp.concatenate([upper, upper, lower], axis=0),
                preferred_element_type=jnp.float32,
            )
            for at in range(many):
                part = both[at * NODES : (at + 1) * NODES, :]
                down[i + at], down[i + at + NP // 2] = part[:, :width], part[:, width:]
        for j in range(NP):
            parts = derived([flow[node_rows(v, i, j), :] for i in range(NP)])
            for i, part in enumerate(parts):
                rows = node_rows(v, i, j)
                rate[rows, :] = rate[rows, :] + part + down[i][j * NP : (j + 1) * NP, :]


def lift_all(state, view, traces, place, orient, rate):
    width = state.shape[1]
    upper, lower = pieces_pair(traces.T)
    sides = jnp.concatenate([upper, lower], axis=0)
    outer = jnp.dot(sides, place[...], preferred_element_type=jnp.float32)
    outer = outer[:ROWS] + outer[ROWS:]
    for which in range(6):
        rows = pl.ds(which * ROWS, ROWS)
        view[rows, :] = view[rows, :] + outer[:, which * width : (which + 1) * width]
    ahead = lax.broadcasted_iota(jnp.int32, (NP, width), 0)
    for which in range(6):
        direction, end = face_rows(which)
        normal = 2.0 * (which % 2) - 1.0
        lanes = pl.ds(which * width, width)
        orients = jnp.broadcast_to(orient[0:1, lanes], (NP, width))
        crossed = (orients & 1) == 1
        turned = orients >= 2
        order = jnp.where(turned, NP - 1 - ahead, ahead)

        def rows_of(v, row):
            base = v * NP * NODES
            if direction == 0:
                return pl.ds(base + end * NODES + row * NP, NP)
            if direction == 1:
                return pl.ds(base + row * NODES + end * NP, NP)
            return pl.ds(base + row * NODES + end, NP, stride=NP)

        for near in range(NP // 2):
            pair = [near, NP - 1 - near]
            far = [[], []]
            for v in range(NV):
                base = which * ROWS + v * NODES
                seen = [
                    jnp.where(
                        crossed,
                        view[pl.ds(base + row, NP, stride=NP), :],
                        view[pl.ds(base + row * NP, NP), :],
                    )
                    for row in pair
                ]
                for half in range(2):
                    picked = jnp.where(turned, seen[1 - half], seen[half])
                    far[half].append(
                        jnp.take_along_axis(picked, order, axis=0, mode="promise_in_bounds")
                    )
            for half in range(2):
                rows = [rows_of(v, pair[half]) for v in range(NV)]
                own = [state[rows[v], :] for v in range(NV)]
                own_flux = flux(own, *primitive(own), direction)
                far_flux = flux(far[half], *primitive(far[half]), direction)
                for v in range(NV):
                    carried = (0.5 * normal * lift_factor) * (far_flux[v] - own_flux[v])
                    gap = (0.5 * penalty * lift_factor) * (far[half][v] - own[v])
                    rate[rows[v], :] = rate[rows[v], :] + (gap - carried)


def table_rows(ref, fill):
    row = ref[...].astype(jnp.float32)
    extra = -row.shape[1] % 128
    if extra > 0:
        row = jnp.concatenate([row, jnp.full((1, extra), fill, jnp.float32)], axis=1)
    return row


def fill_tables(peers, matches, slots, partner, inner, send, place):
    faces = partner.shape[1]
    pack = 16

    def some(at, carry):
        base = pl.multiple_of(at * pack, pack)
        ids = lax.broadcasted_iota(jnp.int32, (pack, faces), 0) + base
        lane = lax.broadcasted_iota(jnp.int32, (pack, faces), 1)
        mate = jnp.broadcast_to(partner[...], (pack, faces))
        hit = jnp.where((ids == mate) & (mate != lane), 1.0, 0.0)
        inner[pl.ds(base, pack), :] = hit.astype(jnp.bfloat16)
        return carry

    lax.fori_loop(0, faces // pack, some, 0)
    peer = table_rows(peers, -1.0)
    match = table_rows(matches, -1.0)
    slot = table_rows(slots, -1.0)
    count = peer.shape[1]
    square = (count, count)
    peer_across = jnp.broadcast_to(peer, square)
    match_across = jnp.broadcast_to(match, square)
    same = peer_across.T == peer_across
    lower = match_across.T < match_across
    sooner = lax.broadcasted_iota(jnp.int32, square, 0) < lax.broadcasted_iota(jnp.int32, square, 1)
    slot_of = lax.broadcasted_iota(jnp.int32, (faces, count), 0).astype(jnp.float32)
    at_slot = jnp.where(slot_of == jnp.broadcast_to(slot, (faces, count)), 1.0, 0.0)
    at_slot = at_slot.astype(jnp.bfloat16)
    places = send.shape[0]
    spots = lax.broadcasted_iota(jnp.int32, (places, count), 0).astype(jnp.float32)
    for ahead, table in ((lower, send), (sooner, place)):
        rank = jnp.sum(jnp.where(same & ahead, 1.0, 0.0), axis=0, keepdims=True)
        spot = jnp.broadcast_to(peer * FCAP + rank, (places, count))
        onehot = jnp.where(spots == spot, 1.0, 0.0).astype(jnp.bfloat16)
        routed = lax.dot_general(
            onehot, at_slot, (((1,), (1,)), ((), ())), preferred_element_type=jnp.float32
        )
        table[...] = routed.astype(jnp.bfloat16)


def window_kernel(*refs):
    fields, refs = refs[:5], refs[5:]
    indices, refs = refs[:6], refs[6:]
    out, refs = refs[0], refs[1:]
    states, rates, older, old, refs = refs[0], refs[1], refs[2], refs[3], refs[4:]
    held, refs = refs[:6], refs[6:]
    inner, send, place, spread, flow, high, low, view, refs = *refs[:8], refs[8:]
    parcels, landings, refs = refs[:2], refs[2:4], refs[4:]
    buffer, traces, send_sem, recv_sem, load_sem, table_sem, pass_send, pass_recv = refs
    peers, matches, slots, partner, orient, blocks = held
    tiles = lax.axis_size("tile")
    me = lax.axis_index("tile")
    level = lax.axis_index("level")
    base_level = level == 0
    upper = (level > 0).astype(jnp.float32)
    other = {"level": 1 - level}
    barrier = pltpu.get_barrier_semaphore()
    parts = [
        (fields[0], 0, CELLS),
        (fields[1], CELLS, 3 * CELLS),
        (fields[2], 4 * CELLS, CELLS),
    ]

    def peer(offset):
        return {"tile": lax.rem(me + offset, tiles)}

    def swap(stage, offset):
        return pltpu.make_async_remote_copy(
            src_ref=buffer.at[stage, lax.rem(me + offset, tiles)],
            dst_ref=traces.at[stage, me],
            send_sem=send_sem.at[stage, offset],
            recv_sem=recv_sem.at[stage, offset],
            device_id=peer(offset),
            device_id_type=pl.DeviceIdType.MESH,
        )

    def portion(at, offset):
        return pltpu.make_async_remote_copy(
            src_ref=parcels[at].at[lax.rem(me + offset, tiles)],
            dst_ref=landings[at].at[me],
            send_sem=send_sem.at[TSTEPS + at, offset],
            recv_sem=recv_sem.at[TSTEPS + at, offset],
            device_id=peer(offset),
            device_id_type=pl.DeviceIdType.MESH,
        )

    def handed(at):
        ref, base, count = parts[at]
        return pltpu.make_async_remote_copy(
            src_ref=ref,
            dst_ref=states.at[2, pl.ds(base, count), :],
            send_sem=pass_send.at[at],
            recv_sem=pass_recv.at[at],
            device_id=other,
            device_id_type=pl.DeviceIdType.MESH,
        )

    def forwarded(stage):
        return pltpu.make_async_remote_copy(
            src_ref=traces.at[stage],
            dst_ref=traces.at[TSTEPS + stage],
            send_sem=pass_send.at[3 + stage],
            recv_sem=pass_recv.at[3 + stage],
            device_id=other,
            device_id_type=pl.DeviceIdType.MESH,
        )

    def greet(offset, carry):
        pl.semaphore_signal(
            barrier, inc=1, device_id=peer(offset), device_id_type=pl.DeviceIdType.MESH
        )
        return carry

    pl.semaphore_signal(barrier, inc=1, device_id=other, device_id_type=pl.DeviceIdType.MESH)
    lax.fori_loop(1, tiles, greet, 0)
    tables = [
        pltpu.make_async_copy(ref, kept, table_sem.at[at])
        for at, (ref, kept) in enumerate(zip(indices, held))
    ]
    loads = [
        pltpu.make_async_copy(ref, states.at[0, pl.ds(base, count), :], load_sem.at[at])
        for at, (ref, base, count) in enumerate(parts)
    ]
    loads.append(pltpu.make_async_copy(fields[3], older, load_sem.at[3]))
    loads.append(pltpu.make_async_copy(fields[4], old, load_sem.at[4]))
    for load in tables + loads:
        load.start()
    pl.semaphore_wait(barrier, tiles)

    @pl.when(base_level)
    def _():
        for at in range(3):
            handed(at).start()

    for load in tables:
        load.wait()
    fill_tables(peers, matches, slots, partner, inner, send, place)
    for stage in range(TSTEPS):
        traces[stage, me] = jnp.zeros(traces.shape[2:], jnp.float32)
    for landing in landings:
        landing[me] = jnp.zeros(landing.shape[1:], jnp.float32)
    for load in loads:
        load.wait()

    def arrive(stage):
        def finish(offset, carry):
            swap(stage, offset).wait()
            return carry

        lax.fori_loop(1, tiles, finish, 0)

    def sweep(work):
        rows = SIZE // 8

        def chunk(at, carry):
            work(pl.ds(pl.multiple_of(at * rows, rows), rows))
            return carry

        lax.fori_loop(0, 8, chunk, 0)

    def share_out(at, state, variables):
        spread_traces(state, spread, variables)
        leave = None
        for half in range(2):
            rows = pl.ds(half * ROWS + variables[0] * NODES, len(variables) * NODES)
            part = lax.dot_general(
                send[...], spread[rows, :], (((1,), (1,)), ((), ())),
                preferred_element_type=jnp.float32,
            )
            leave = part if leave is None else leave + part
        parcels[at][...] = leave.reshape(parcels[at].shape)

        def begin(offset, carry):
            portion(at, offset).start()
            return carry

        lax.fori_loop(1, tiles, begin, 0)

    def collect(at):
        def finish(offset, carry):
            portion(at, offset).wait()
            return carry

        lax.fori_loop(1, tiles, finish, 0)

    def step(t, carry):
        def on(base, at):
            return pl.when((level == 0) & (t == at) if base else (level > 0) & (t == at))

        state, rate = states.at[t], rates.at[t]
        stage = jnp.where(t <= 1, t, 2)
        leaving = jnp.where(base_level, t <= 2, (t <= 1) | (t == 4))
        lasting = jnp.where(base_level, t <= 2, (t != 1) & (t != 4))

        @on(False, 2)
        def _():
            for at in range(2):
                handed(at).wait_recv()
            share_out(0, state, range(NV - 1))
            handed(2).wait_recv()
            share_out(1, state, range(NV - 1, NV))

        @pl.when((leaving | lasting) & (base_level | (t != 2)))
        def _():
            spread_traces(state, spread)

        @pl.when(leaving)
        def _():
            leave = lax.dot_general(
                send[...], spread[...], (((1,), (1,)), ((), ())), preferred_element_type=jnp.float32
            )
            leave = leave[:, :ROWS] + leave[:, ROWS:]
            buffer[stage] = leave.reshape(tiles, FCAP, ROWS)

            def begin(offset, carry):
                swap(stage, offset).start()
                return carry

            lax.fori_loop(1, tiles, begin, 0)

        @pl.when(lasting)
        def _():
            planes_and_views(state, spread, inner, flow, high, low, rate, view)
            remaining_volume(flow, high, low, blocks, rate)

            @pl.when(base_level | (t == 0))
            def _():
                arrive(stage)

            @on(True, 2)
            def _():
                for at in range(3):
                    handed(at).wait_send()
                forwarded(1).start()
                forwarded(2).start()

            @on(False, 2)
            def _():
                for at in range(2):
                    collect(at)
                traces[TSTEPS] = jnp.concatenate(
                    [landing[...] for landing in landings], axis=2
                )

            @on(False, 3)
            def _():
                arrive(1)
                forwarded(1).wait_recv()

            @on(False, 6)
            def _():
                forwarded(2).wait_recv()

            @on(False, 7)
            def _():
                arrive(2)

            own = jnp.where(
                base_level | (t == 0),
                t,
                jnp.where(t == 3, 1, jnp.where(t == 7, 2, jnp.where(t == 2, 3, t - 1))),
            )
            mixed = (level > 0) & ((t == 3) | (t == 7))
            newer = jnp.where(mixed, jnp.where(t == 3, 4, 5), own)
            elder = jnp.where(mixed, newer - 1, own)
            share = jnp.where(mixed, weight_next, 0.0)
            seen = traces[own] + share * (traces[newer] - traces[elder])
            lift_all(state, view, seen.reshape(tiles * FCAP, ROWS), place, orient, rate)

        @pl.when(t == 0)
        def _():
            def work(rows):
                extra = weight_back * older[rows, :] + (weight_here - 1.0) * old[rows, :]
                states[1, rows, :] = states[0, rows, :] + step_size * (
                    rates[0, rows, :] + upper * extra
                )

            sweep(work)

        @on(True, 1)
        def _():
            def work(rows):
                states[2, rows, :] = states[1, rows, :] + step_size * rates[1, rows, :]

            sweep(work)

        @on(True, 2)
        def _():
            def work(rows):
                moved = states[2, rows, :] + step_size * rates[2, rows, :] - states[0, rows, :]
                out[rows, :] = moved * SCALE

            sweep(work)

        @on(False, 2)
        def _():
            def work(rows):
                below = step_size * rates[2, rows, :]
                states[3, rows, :] = states[1, rows, :] + weight_next * below
                states[5, rows, :] = states[2, rows, :] + below

            sweep(work)

        @on(False, 3)
        def _():
            def work(rows):
                states[4, rows, :] = states[3, rows, :] + step_size * (
                    rates[3, rows, :]
                    + weight_back * old[rows, :]
                    + (weight_here - 1.0) * rates[2, rows, :]
                )

            sweep(work)

        @on(False, 5)
        def _():
            def work(rows):
                below = step_size * rates[5, rows, :]
                states[7, rows, :] = states[4, rows, :] + weight_next * below
                states[6, rows, :] = states[5, rows, :] + below

            sweep(work)

        @on(False, 7)
        def _():
            def work(rows):
                change = (
                    rates[7, rows, :]
                    + weight_back * rates[2, rows, :]
                    + (weight_here - 1.0) * rates[5, rows, :]
                    + weight_next * rates[6, rows, :]
                )
                moved = states[7, rows, :] + step_size * change - states[0, rows, :]
                out[rows, :] = moved * SCALE

            sweep(work)

        return carry

    lax.fori_loop(0, STEPS, step, 0)

    @pl.when(base_level)
    def _():
        for stage in range(1, TSTEPS):
            forwarded(stage).wait_send()


def window_of(fields, indices):
    tiles = lax.axis_size("tile")
    width = fields[0].shape[1]
    faces = indices[3].shape[1]
    full = (SIZE, width)
    f32, bf16 = jnp.float32, jnp.bfloat16
    operands = [*fields, *indices, jnp.asarray(block_numbers())]
    operands = [pltpu.with_memory_space_constraint(x, pltpu.HBM) for x in operands]
    return pl.pallas_call(
        window_kernel,
        out_shape=jax.ShapeDtypeStruct(full, f32),
        in_specs=[pl.BlockSpec(memory_space=pl.ANY)] * len(operands),
        out_specs=VMEM,
        scratch_shapes=[
            pltpu.VMEM((STEPS,) + full, f32),
            pltpu.VMEM((STEPS,) + full, f32),
            pltpu.VMEM(full, f32),
            pltpu.VMEM(full, f32),
            *[pltpu.VMEM(x.shape, x.dtype) for x in operands[5:]],
            pltpu.VMEM((faces, faces), bf16),
            pltpu.VMEM((tiles * FCAP, faces), bf16),
            pltpu.VMEM((tiles * FCAP, faces), bf16),
            pltpu.VMEM((2 * ROWS, faces), bf16),
            pltpu.VMEM(full, f32),
            pltpu.VMEM(full, bf16),
            pltpu.VMEM(full, bf16),
            pltpu.VMEM((6 * ROWS, width), f32),
            *[pltpu.VMEM((tiles, FCAP, many * NODES), f32) for many in (NV - 1, 1, NV - 1, 1)],
            pltpu.VMEM((TSTEPS, tiles, FCAP, ROWS), f32),
            pltpu.VMEM((2 * TSTEPS, tiles, FCAP, ROWS), f32),
            pltpu.SemaphoreType.DMA((TSTEPS + 2, tiles)),
            pltpu.SemaphoreType.DMA((TSTEPS + 2, tiles)),
            pltpu.SemaphoreType.DMA((5,)),
            pltpu.SemaphoreType.DMA((6,)),
            pltpu.SemaphoreType.DMA((6,)),
            pltpu.SemaphoreType.DMA((6,)),
        ],
        compiler_params=pltpu.CompilerParams(
            collective_id=2, has_side_effects=True, vmem_limit_bytes=44 << 20
        ),
    )(*operands)


def turning():
    nodes = np.arange(NODES)
    blocks = []
    for orient in range(4):
        source = nodes.reshape(NP, NP)
        if orient >= 2:
            source = source[::-1, ::-1]
        if orient % 2 == 1:
            source = source.T
        block = np.zeros((NODES, NODES), np.float32)
        block[nodes, source.reshape(-1)] = 1.0
        blocks.append(block)
    return np.concatenate(blocks, axis=1)


def body(
    density,
    momentum,
    energy,
    rhs_older,
    rhs_old,
    peer_tile,
    peer_index,
    boundary_slot,
    face_partner,
    face_orient,
):
    width = density.shape[-1]
    if lax.axis_size("level") == 2:
        fields = [density, momentum, energy, rhs_older, rhs_old]
        indices = [peer_tile, peer_index, boundary_slot, face_partner, face_orient]
        result = window_of([field.reshape(-1, width) for field in fields], indices)
        return result.reshape(rhs_old.shape)
    start = jnp.concatenate(
        [
            density.reshape(-1, width),
            momentum.reshape(-1, width),
            energy.reshape(-1, width),
        ],
        axis=0,
    )
    level = lax.axis_index("level")
    tiles = lax.axis_size("tile")
    peers = peer_tile[0]
    matches = peer_index[0]
    slots = boundary_slot[0]
    partner = face_partner[0]
    orient = face_orient[0]
    count = peers.shape[0]
    faces = partner.shape[0]
    same_peer = peers[:, None] == peers[None, :]
    listing = jnp.arange(count, dtype=jnp.int32)
    send_rank = jnp.sum(same_peer & (matches[None, :] < matches[:, None]), axis=1, dtype=jnp.int32)
    recv_rank = jnp.sum(same_peer & (listing[None, :] < listing[:, None]), axis=1, dtype=jnp.int32)
    places = jnp.arange(tiles * FCAP, dtype=jnp.int32)
    ids = jnp.arange(faces, dtype=jnp.int32)
    exact = jnp.bfloat16
    at_slot = (slots[:, None] == ids[None, :]).astype(exact)

    def routing(rank):
        onehot = (places[:, None] == (peers * FCAP + rank)[None, :]).astype(exact)
        return jnp.dot(onehot, at_slot, preferred_element_type=jnp.float32).astype(exact)

    send = routing(send_rank)
    place = routing(recv_rank)
    inner = ((ids[:, None] == partner[None, :]) & (partner != ids)[None, :]).astype(exact)
    masks = (orient[None, :] == jnp.arange(8, dtype=jnp.int32)[:, None]).astype(jnp.float32)
    turn = jnp.asarray(turning(), exact)
    numbers = derivative_numbers()
    diagonals = np.stack(
        [
            np.stack([-metric * numbers[k, (k + shift) % NP] for k in range(NP)])
            for shift in range(NP)
        ]
    ).astype(np.float32)
    rolled = jnp.broadcast_to(jnp.asarray(diagonals)[:, :, None], (NP, NP, width))

    tables = (masks, turn, inner, send, place, rolled)

    def rates(states):
        return rates_of(states, tables)

    older = rhs_older.reshape(-1, width)
    old = rhs_old.reshape(-1, width)

    def advance(state, own_rate, older, old, below):
        corrected = (
            state
            + step_size * (own_rate - old)
            + step_size * (weight_back * older + weight_here * old + weight_next * below)
        )
        return jnp.where(level == 0, state + step_size * own_rate, corrected)

    state = start
    for repeat in range(TSTEPS):
        own_rate = rates([state])[0]
        below = shifted(own_rate, "level", 1)
        state = advance(state, own_rate, older, old, below)
        older = old
        old = below
    return ((state - start) / (TSTEPS * step_size)).reshape(rhs_old.shape)


def solution(mesh):
    return jax.shard_map(
        body,
        mesh=mesh,
        in_specs=(
            P("level", None, None, None, "tile"),
            P("level", None, None, None, None, "tile"),
            P("level", None, None, None, "tile"),
            P("level", None, None, None, None, "tile"),
            P("level", None, None, None, None, "tile"),
            P("tile", None),
            P("tile", None),
            P("tile", None),
            P("tile", None),
            P("tile", None),
        ),
        out_specs=P("level", None, None, None, None, "tile"),
        check_vma=False,
    )
```
